512 devices in a mesh: blk: 128 (over y_hi, z, x), feat: 4 (over y_lo, core).
Axes of the slice: x: 4, y: 4 (y_hi: 2, y_lo: 2; y = y_hi * 2 + y_lo), z: 16, core: 2. Of those that a mesh axis runs over, the one named last changes fastest.
Arguments:
- features: bfloat16 [256, 131072], P('feat', 'blk'), may hold values from -6 to 6
- block_values: bfloat16 [17408, 128, 128], P('blk'), may hold values from 0 to 1, as said below
- block_rows: int32 [17408], P('blk'), may hold values from 0 to 7, as said below
- block_cols: int32 [17408], P('blk'), may hold values from 0 to 1023, as said below
- block_count: int32 [128], P('blk'), may hold values from 8 to 136, as said below
- labels: int32 [131072], P(('blk', 'feat')), may hold values from 0 to 127
- weight_in: bfloat16 [256, 256], replicated, may hold values from -0.375 to 0.375
- weight_out: bfloat16 [256, 128], replicated, may hold values from -1 to 1
Outputs:
- logits: float32 [128, 131072], P(None, ('blk', 'feat'))
- grad_in: float32 [256, 256], replicated
- grad_out: float32 [256, 128], replicated
The draws below stay inside these ranges and needn't reach their ends.
Inputs may be any that keep to these rules, and one draw needn't show every extreme that they name: The first block_count[s] slots of stripe s are its blocks; the remaining slots hold blocks that are not part of the matrix; every stripe holds its 8 diagonal blocks, and the busiest stripe fills all 136 slots. `block_rows`: block row of a slot inside its stripe. `block_cols`: every slot's block column lies within 8 blocks of its global block row, counted around the loop of 1024 block columns; the live slots of a stripe name distinct blocks. `block_values`: the matrix assembled from the live slots is symmetric: live block (r, c) is the transpose of live block (c, r).
All inputs are finite; a program needn't handle non-finite values.
Results may differ from the reference program's by a relative error of at most 0.002.
The reference program's roundings to bfloat16 on the way count: a program that leaves them out, or rounds other values in their place, can miss the bound.
Values may be sent and summed in bfloat16 or wider, within the bound.
No kernel may reach another device: no remote copies, remote signals or barrier semaphores. Data moves between devices by JAX's collectives and lax.ppermute only.
A program may use at most 64 MiB of HBM per device.

```python
import math
import jax
import jax.numpy as jnp
from jax import lax

BS = 128
BROWS = 8
BAND = 1
IN = 256
HID = 256
CLS = 128
BLOCKS = 1024
NODES = 131072
SLOTS = 136


def arrange(grid, order, stripe_total):
    return jnp.take_along_axis(grid.reshape(stripe_total, SLOTS), order, axis=1)


def band_layout(key):
    stripe_total = BLOCKS // BROWS
    reach_blocks = BAND * BROWS
    span_blocks = 2 * reach_blocks + 1
    shifts = jax.random.randint(jax.random.fold_in(key, 11), (stripe_total,), 0, 6)
    density = 1000 // jnp.left_shift(jnp.ones_like(shifts), shifts)
    hottest = jax.random.randint(jax.random.fold_in(key, 12), (), 0, stripe_total)
    density = jnp.where(jnp.arange(stripe_total) == hottest, 1000, density)
    row_ids = jnp.arange(BLOCKS)
    distance = jnp.arange(reach_blocks + 1)
    partner = (row_ids[:, None] + distance[None, :]) % BLOCKS
    threshold = jnp.maximum(density[row_ids // BROWS][:, None], density[partner // BROWS])
    rolled = jax.random.randint(jax.random.fold_in(key, 13), (BLOCKS, reach_blocks + 1), 0, 1000)
    upper = (rolled < threshold) | (distance[None, :] == 0)
    stripe_ids = jnp.arange(stripe_total)
    local_rows = jnp.arange(BROWS)
    offsets = jnp.arange(span_blocks) - reach_blocks
    local_grid = local_rows[None, :, None] + 0 * stripe_ids[:, None, None] + 0 * offsets[None, None, :]
    global_rows = stripe_ids[:, None, None] * BROWS + local_grid
    global_cols = (global_rows + offsets[None, None, :]) % BLOCKS
    base_rows = jnp.where(offsets[None, None, :] >= 0, global_rows, global_cols)
    base_dist = jnp.abs(offsets)[None, None, :] + 0 * global_rows
    flipped = (offsets[None, None, :] < 0) & (global_rows >= 0)
    present = upper[base_rows, base_dist]
    present_grid = present.reshape(stripe_total, SLOTS)
    random_keys = jax.random.randint(jax.random.fold_in(key, 14), (stripe_total, SLOTS), 0, 1048576)
    sort_keys = jnp.where(present_grid, 0, 1073741824) + random_keys * SLOTS + jnp.arange(SLOTS)[None, :]
    order = jnp.argsort(sort_keys, axis=1)
    counts = jnp.sum(present_grid.astype(jnp.int32), axis=1)
    return (arrange(local_grid, order, stripe_total), arrange(global_cols, order, stripe_total), arrange(base_rows, order, stripe_total), arrange(base_dist, order, stripe_total), arrange(flipped, order, stripe_total), counts)


def draw_block_rows(key, part):
    return band_layout(key)[0].reshape(-1).astype(jnp.int32)


def draw_block_cols(key, part):
    return band_layout(key)[1].reshape(-1).astype(jnp.int32)


def draw_block_count(key, part):
    return band_layout(key)[5].astype(jnp.int32)


def draw_block_values(key, part):
    layout = band_layout(key)
    base_rows = layout[2]
    base_dist = layout[3]
    flipped = layout[4]
    reach_blocks = BAND * BROWS
    base = jax.random.uniform(jax.random.fold_in(key, 15), (BLOCKS, reach_blocks + 1, BS, BS), jnp.float32)
    mirrored = 0.5 * (base + jnp.swapaxes(base, 2, 3))
    base = jnp.where((jnp.arange(reach_blocks + 1) == 0)[None, :, None, None], mirrored, base)
    chosen = base[base_rows, base_dist]
    chosen = jnp.where(flipped[:, :, None, None], jnp.swapaxes(chosen, 2, 3), chosen)
    factor = 1.0 / math.sqrt(BS * (reach_blocks + 1))
    return (chosen * factor).reshape(BLOCKS // BROWS * SLOTS, BS, BS).astype(jnp.bfloat16)


def draw_weight_out(key, part):
    normal = jax.random.normal(jax.random.fold_in(key, 21), (HID, CLS), jnp.float32)
    base = jnp.clip(normal, -6.0, 6.0) / math.sqrt(HID)
    return base.astype(jnp.bfloat16)


def with_ends(drawn, rng, least, top_value):
    shape = drawn.shape
    index_at = [jax.random.randint(jax.random.fold_in(rng, axis), (), 0, shape[axis]) for axis in range(len(shape))]
    drawn = drawn.at[tuple(index_at)].set(least)
    longest = shape.index(max(shape))
    index_at[longest] = (index_at[longest] + 1) % shape[longest]
    return drawn.at[tuple(index_at)].set(top_value)


def block_levels(stream_key, shape, pieces, low, high):
    def one(axis_at, blocks):
        steps = jax.random.uniform(jax.random.fold_in(jax.random.fold_in(stream_key, 6), axis_at), (blocks,), jnp.float32, low / len(pieces), high / len(pieces))
        return jnp.repeat(jnp.exp(steps), shape[axis_at] // blocks).reshape((-1,) + (1,) * (len(shape) - axis_at - 1))

    level = one(*pieces[0])
    for cut in pieces[1:]:
        level = level * one(*cut)
    return level


def noise(rng, dims, deviation, bound, pieces=(), kind=jnp.bfloat16):
    factor_of = block_levels(rng, dims, pieces, -0.22, 0.18) if pieces else 1.0
    values = jax.random.normal(rng, dims, jnp.float32) * deviation * factor_of
    return jnp.minimum(jnp.maximum(values, -bound), bound).astype(kind)


def setup_inputs(seed: int = 0) -> dict:
    key_of = jax.random.split(jax.random.key(seed), 9)
    return {
        "features": noise(key_of[0], (IN, NODES), 1.0, 6.0, ((0, 4), (1, 128))),
        "block_values": draw_block_values(jax.random.fold_in(key_of[8], 71), 0),
        "block_rows": draw_block_rows(jax.random.fold_in(key_of[8], 71), 0),
        "block_cols": draw_block_cols(jax.random.fold_in(key_of[8], 71), 0),
        "block_count": draw_block_count(jax.random.fold_in(key_of[8], 71), 0),
        "labels": with_ends(jax.random.randint(key_of[5], (NODES,), 0, CLS), jax.random.fold_in(key_of[5], 1), 0, CLS - 1).astype(jnp.int32),
        "weight_in": noise(key_of[6], (IN, HID), IN ** -0.5, 0.375),
        "weight_out": draw_weight_out(jax.random.fold_in(key_of[8], 71), 0),
    }


def propagate(matrix, block_values, block_rows, block_cols, block_count):
    columns = matrix.shape[1]
    blocked = matrix.reshape(BLOCKS, BS, columns).astype(jnp.float32)
    stripe_total = BLOCKS // BROWS
    values = block_values.reshape(stripe_total, SLOTS, BS, BS)
    rows_all = block_rows.reshape(stripe_total, SLOTS)
    cols_all = block_cols.reshape(stripe_total, SLOTS)

    def stripe_product(packed):
        stripe_values, stripe_rows, stripe_cols, stripe_count = packed
        gathered = jnp.take(blocked, stripe_cols.astype(jnp.int32), axis=0)
        products = jnp.einsum('sab,sbc->sac', stripe_values.astype(jnp.float32), gathered, precision=lax.Precision.HIGHEST)
        live_slots = jnp.arange(SLOTS, dtype=jnp.int32) < stripe_count
        placing = ((stripe_rows[:, None] == jnp.arange(BROWS, dtype=jnp.int32)[None, :]) & live_slots[:, None]).astype(jnp.float32)
        placed = jnp.einsum('sr,sac->rac', placing, products, precision=lax.Precision.HIGHEST)
        return placed.reshape(BROWS * BS, columns)
    stacked = lax.map(stripe_product, (values, rows_all, cols_all, block_count))
    return stacked.reshape(NODES, columns)

def reference(features, block_values, block_rows, block_cols, block_count, labels, weight_in, weight_out):
    inputs = features.T
    prop_in = propagate(inputs, block_values, block_rows, block_cols, block_count).astype(jnp.bfloat16)
    pre_hidden = jnp.dot(prop_in, weight_in, preferred_element_type=jnp.float32)
    hidden = jax.nn.gelu(pre_hidden, approximate=True).astype(jnp.bfloat16)
    prop_hid = propagate(hidden, block_values, block_rows, block_cols, block_count).astype(jnp.bfloat16)
    logit_rows = jnp.dot(prop_hid, weight_out, preferred_element_type=jnp.float32)
    shifted = logit_rows - lax.optimization_barrier(jnp.max(logit_rows, axis=1, keepdims=True))
    exponent = jnp.exp(shifted)
    probability = exponent / lax.optimization_barrier(jnp.sum(exponent, axis=1, keepdims=True))
    onehot = (labels[:, None] == jnp.arange(CLS, dtype=jnp.int32)[None, :]).astype(jnp.float32)
    dlogits = ((probability - onehot) * (1.0 / math.sqrt(NODES))).astype(jnp.bfloat16)
    grad_out = jnp.dot(prop_hid.T, dlogits, preferred_element_type=jnp.float32)
    spread = propagate(dlogits, block_values, block_rows, block_cols, block_count)
    back_hid = jnp.dot(spread, weight_out.T.astype(jnp.float32), precision=lax.Precision.HIGHEST)

    def activation(entry_value):
        return jax.nn.gelu(entry_value, approximate=True)
    unused_output, pullback = jax.vjp(activation, pre_hidden)
    grad_pre = pullback(back_hid)[0].astype(jnp.bfloat16)
    grad_in = jnp.dot(prop_in.T, grad_pre, preferred_element_type=jnp.float32)
    return (logit_rows.T, grad_in, grad_out)
```

```python
import functools
import math

import jax
import jax.numpy as jnp
from jax import lax
from jax.experimental import pallas as pl
from jax.experimental.pallas import tpu as pltpu
from jax.sharding import Mesh
from jax.sharding import PartitionSpec as P

BLK = ("yh", "z", "x")
FEAT = ("yl", "co")
PLANE = ("yh", "x")
F32 = jnp.float32
BF16 = jnp.bfloat16
BS = 128
WIDTH = 18 * BS
TILE = 2 * BS
NT = (((1,), (1,)), ((), ()))
NN = (((1,), (0,)), ((), ()))
TN = (((0,), (0,)), ((), ()))
GELU_A = math.sqrt(2.0 / math.pi)
GELU_B = 0.044715


def dot(a, b, dims):
    return lax.dot_general(a, b, dims, preferred_element_type=F32)


def params(mib):
    return pltpu.CompilerParams(vmem_limit_bytes=mib << 20)


def whole():
    return pl.BlockSpec(memory_space=pltpu.VMEM)


def sds(shape, dtype):
    return jax.ShapeDtypeStruct(shape, dtype)


def assemble_kernel(per_step, rows_ref, cols_ref, count_ref, blocks_ref, dense_ref):
    step = pl.program_id(0)
    stripe_blocks = dense_ref.shape[0] // BS
    total_blocks = stripe_blocks * lax.axis_size(BLK)
    first = (lax.axis_index(BLK) - 1) * stripe_blocks - total_blocks

    @pl.when(step == 0)
    def _():
        dense_ref[...] = jnp.zeros_like(dense_ref)

    for j in range(per_step):
        slot = step * per_step + j

        @pl.when(slot < count_ref[0])
        def _():
            row = rows_ref[slot]
            local = lax.rem(cols_ref[slot] - first, total_blocks)
            col = local - (row // 2) * 2
            row = pl.multiple_of(row * BS, BS)
            col = pl.multiple_of(col * BS, BS)
            dense_ref[pl.ds(row, BS), pl.ds(col, BS)] = blocks_ref[j]


def assemble(block_values, rows, cols, count, stripe_rows):
    slots = block_values.shape[0]
    per_step = 17
    return pl.pallas_call(
        functools.partial(assemble_kernel, per_step),
        grid_spec=pltpu.PrefetchScalarGridSpec(
            num_scalar_prefetch=3,
            grid=(slots // per_step,),
            in_specs=[pl.BlockSpec((per_step, BS, BS), lambda i, *_: (i, 0, 0))],
            out_specs=pl.BlockSpec((stripe_rows, WIDTH), lambda i, *_: (0, 0)),
        ),
        out_shape=sds((stripe_rows, WIDTH), BF16),
        compiler_params=params(24),
        name="assemble",
    )(rows, cols, count, pltpu.with_memory_space_constraint(block_values, pltpu.HBM))


def band_product(left, own, right, dense, t):
    stripe = own.shape[1]
    band = dense.at[pl.ds(t * TILE, TILE)]
    cut = stripe - t * TILE
    acc = dot(left[:, t * TILE :], band[:, :cut], NT)
    acc = acc + dot(own[...], band[:, cut : cut + stripe], NT)
    return acc + dot(right[:, : (t + 1) * TILE], band[:, cut + stripe :], NT)


def tiles_of(stripe):
    return [(t, slice(t * TILE, (t + 1) * TILE)) for t in range(stripe // TILE)]


def prop_in_kernel(left, own, right, labels, dense, out):
    channels = own.shape[0]
    tag = jnp.broadcast_to(labels[...].astype(F32), (16, labels.shape[1])).astype(BF16)
    for t, at in tiles_of(own.shape[1]):
        out[:channels, at] = band_product(left, own, right, dense, t).astype(BF16)
        out[channels:, at] = tag if t == 0 else jnp.zeros_like(tag)


def prop_kernel(left, own, right, dense, out):
    for t, at in tiles_of(own.shape[1]):
        out[:, at] = band_product(left, own, right, dense, t).astype(BF16)


def hidden_kernel(first, second, third, fourth, w_in, hidden, pre_own, prop_in, labels):
    yl = lax.axis_index("yl")
    co = lax.axis_index("co")
    hid = hidden.shape[0]
    half = hid // 2
    depth = prop_in.shape[0] // 4
    for part, dy, dc in ((first, 0, 0), (second, 0, 1), (third, 1, 0), (fourth, 1, 1)):
        place = (yl + dy - 2 * yl * dy) * 2 + (co + dc - 2 * co * dc)
        rows = pl.ds(pl.multiple_of(place * depth, depth), depth)
        prop_in[rows, :] = part[:depth, :]
        labels[:, pl.ds(pl.multiple_of(place * TILE, TILE), TILE)] = part[
            depth : depth + 8, :TILE
        ].astype(F32)
    weight = w_in[:, pl.ds(pl.multiple_of(co * hid, hid), hid)]
    pre = dot(weight, prop_in[...], TN)
    inner = GELU_A * (pre + GELU_B * (pre * pre * pre))
    hidden[...] = (pre * (0.5 * (1.0 + jnp.tanh(inner)))).astype(BF16)
    pre_own[...] = jnp.where(yl == 0, pre[:half], pre[half:])


def logits_kernel(scale, own, other, w_out, labels, out, dl, share, scores):
    yl = lax.axis_index("yl")
    co = lax.axis_index("co")
    hid = own.shape[0]
    w_own = w_out[pl.ds(pl.multiple_of(co * hid, hid), hid), :]
    w_other = w_out[pl.ds(pl.multiple_of((1 - co) * hid, hid), hid), :]
    logit = dot(w_own, own[...], TN) + dot(w_other, other[...], TN)
    scores[...] = logit
    start = pl.multiple_of((yl * 2 + co) * out.shape[1], out.shape[1])
    out[...] = scores[:, pl.ds(start, out.shape[1])]
    shifted = logit - jnp.max(logit, axis=0, keepdims=True)
    exponent = jnp.exp(shifted)
    probability = exponent / jnp.sum(exponent, axis=0, keepdims=True)
    classes = lax.broadcasted_iota(jnp.int32, logit.shape, 0).astype(F32)
    onehot = jnp.where(classes == labels[0:1, :], 1.0, 0.0)
    dlogits = ((probability - onehot) * scale).astype(BF16)
    dl[...] = dlogits
    rows = share.shape[0]
    mine = own[pl.ds(pl.multiple_of(yl * rows, rows), rows), :]
    share[...] = dot(mine, dlogits, NT)


def grads_kernel(left, own, right, w_out, pre_own, prop_in, share_out, dense, out):
    yl = lax.axis_index("yl")
    co = lax.axis_index("co")
    half = pre_own.shape[0]
    w = w_out[pl.ds(pl.multiple_of((co * 2 + yl) * half, half), half), :]
    share = None
    for t, at in tiles_of(own.shape[1]):
        acc = band_product(left, own, right, dense, t)
        high = acc.astype(BF16)
        rest = acc - high.astype(F32)
        middle = rest.astype(BF16)
        low = (rest - middle.astype(F32)).astype(BF16)
        back = dot(w, high, NN) + (dot(w, middle, NN) + dot(w, low, NN))
        v = pre_own[:, at]
        th = jnp.tanh(GELU_A * (v + GELU_B * (v * v * v)))
        slope = 0.5 * (1.0 + th) + (0.5 * v) * (1.0 - th * th) * (
            GELU_A * (1.0 + (3.0 * GELU_B) * (v * v))
        )
        part = dot((back * slope).astype(BF16), prop_in[:, at], NT)
        share = part if share is None else share + part
    pieces, rows, _ = out.shape
    width = share.shape[1]
    for p in range(pieces):
        out[p, :, :width] = share[p * rows : (p + 1) * rows]
        out[p, :, width:] = share_out[p * rows : (p + 1) * rows]


def sum_kernel(parts, out):
    total = parts[0]
    for p in range(1, parts.shape[0]):
        total = total + parts[p]
    for p in range(out.shape[0]):
        out[p] = total


def collect_kernel(parts, grad_in, grad_out, rows_ref):
    planes = parts.shape[0] // 4
    rows = parts.shape[1]
    width = grad_in.shape[0]
    for p in range(planes):
        for yl in range(2):
            for co in range(2):
                at = ((co * 2 + yl) * planes + p) * rows
                rows_ref[at : at + rows, :] = parts[p * 4 + yl * 2 + co]
    grad_in[...] = rows_ref[:, :width].T
    grad_out[...] = rows_ref[:, width:]


def call(kernel, args, out_shape, name, mib=16, scratch=()):
    many = isinstance(out_shape, (tuple, list))
    return pl.pallas_call(
        kernel,
        in_specs=[whole()] * len(args),
        out_specs=[whole()] * len(out_shape) if many else whole(),
        out_shape=out_shape,
        scratch_shapes=list(scratch),
        compiler_params=params(mib),
        name=name,
    )(*args)


def neighbours(value):
    count = lax.axis_size(BLK)
    left = lax.ppermute(value, BLK, [(i, (i + 1) % count) for i in range(count)])
    right = lax.ppermute(value, BLK, [((i + 1) % count, i) for i in range(count)])
    return left, value, right


def flipped(value, axes):
    shift = {("co",): 1, ("yl",): 2, ("yl", "co"): 3}[axes]
    return lax.ppermute(value, FEAT, [(i, i ^ shift) for i in range(4)])


def on_device(
    features, block_values, block_rows, block_cols, block_count, labels, weight_in, weight_out
):
    devices = lax.axis_size(BLK)
    depth, stripe = features.shape
    node_scale = 1.0 / math.sqrt(devices * stripe)
    hid = weight_in.shape[1]
    classes = weight_out.shape[1]
    mine = labels.shape[0]

    x_pieces = neighbours(features)
    dense = assemble(block_values, block_rows, block_cols, block_count, stripe)
    first = call(
        prop_in_kernel,
        (*x_pieces, labels.reshape(1, mine), dense),
        sds((depth + 16, stripe), BF16),
        "prop_in",
    )
    fourth = flipped(first, ("yl", "co"))
    third = flipped(first, ("yl",))
    second = flipped(first, ("co",))
    hidden, pre_own, prop_in, label_rows = call(
        hidden_kernel,
        (first, second, third, fourth, weight_in),
        (
            sds((hid // 2, stripe), BF16),
            sds((hid // 4, stripe), F32),
            sds((4 * depth, stripe), BF16),
            sds((8, stripe), F32),
        ),
        "hidden",
    )

    prop_own = call(
        prop_kernel, (*neighbours(hidden), dense), sds((hid // 2, stripe), BF16), "prop_hid"
    )
    prop_other = flipped(prop_own, ("co",))
    logits, dl, share_out = call(
        functools.partial(logits_kernel, node_scale),
        (prop_own, prop_other, weight_out, label_rows),
        (
            sds((classes, mine), F32),
            sds((classes, stripe), BF16),
            sds((hid // 4, classes), F32),
        ),
        "logits",
        scratch=[pltpu.VMEM((classes, stripe), F32)],
    )

    plane = lax.axis_size(PLANE)
    rows = hid // 4 // plane
    width = 4 * depth + classes
    share = call(
        grads_kernel,
        (*neighbours(dl), weight_out, pre_own, prop_in, share_out, dense),
        sds((plane, rows, width), F32),
        "grads",
    )
    parts = lax.all_to_all(share, PLANE, 0, 0, tiled=True)
    parts = call(sum_kernel, (parts,), sds((lax.axis_size("z"), rows, width), F32), "sum_plane")
    parts = lax.all_to_all(parts, "z", 0, 0, tiled=True)
    parts = call(sum_kernel, (parts,), sds((plane * 4, rows, width), F32), "sum_z")
    parts = lax.all_to_all(parts, PLANE + FEAT, 0, 0, tiled=True)
    grad_in, grad_out = call(
        collect_kernel,
        (parts,),
        (sds((4 * depth, hid), F32), sds((hid, classes), F32)),
        "collect",
        scratch=[pltpu.VMEM((hid, width), F32)],
    )
    return (logits, grad_in, grad_out)


def solution(mesh):
    fine = Mesh(mesh.devices.reshape(2, 16, 4, 2, 2), BLK + FEAT)
    placed = (
        P(FEAT, BLK),
        P(BLK, None, None),
        P(BLK),
        P(BLK),
        P(BLK),
        P(BLK + FEAT),
        P(),
        P(),
    )
    return jax.shard_map(
        on_device,
        mesh=fine,
        in_specs=placed,
        out_specs=(P(None, BLK + FEAT), P(), P()),
        check_vma=False,
    )
```

```python
import functools
import math

import jax
import jax.numpy as jnp
from jax import lax
from jax.experimental import pallas as pl
from jax.experimental.pallas import tpu as pltpu
from jax.sharding import Mesh
from jax.sharding import PartitionSpec as P


BLK = ("yh", "z", "x")
FEAT = ("yl", "co")
PLANE = ("yh", "x")
F32 = jnp.float32
BF16 = jnp.bfloat16
BS = 128
WIDTH = 18 * BS
TILE = 2 * BS
TAG = 8
NT = (((1,), (1,)), ((), ()))
TN = (((0,), (0,)), ((), ()))
GELU_A = math.sqrt(2.0 / math.pi)
GELU_B = 0.044715


def dot(a, b, dims):
    return lax.dot_general(a, b, dims, preferred_element_type=F32)


def params(mib):
    return pltpu.CompilerParams(vmem_limit_bytes=mib << 20)


def whole():
    return pl.BlockSpec(memory_space=pltpu.VMEM)


def sds(shape, dtype):
    return jax.ShapeDtypeStruct(shape, dtype)


def assemble_kernel(chunks, rows_ref, cols_ref, count_ref, blocks_hbm, dense_ref, blocks, sems):
    slots = blocks.shape[0]
    each = slots // chunks
    copies = [
        pltpu.make_async_copy(
            blocks_hbm.at[pl.ds(i * each, each)], blocks.at[pl.ds(i * each, each)], sems.at[i]
        )
        for i in range(chunks)
    ]
    for copy in copies:
        copy.start()
    spare = dense_ref.shape[0] - BS
    total_blocks = spare // BS * lax.axis_size(BLK)
    first = (lax.axis_index(BLK) - 1) * (spare // BS)
    count = count_ref[0]
    dense_ref[...] = jnp.zeros_like(dense_ref)
    for i in range(chunks):
        copies[i].wait()

        def place(slot, carry):
            row = rows_ref[slot]
            local = cols_ref[slot] - first
            local = jnp.where(local < 0, local + total_blocks, local)
            local = jnp.where(local >= total_blocks, local - total_blocks, local)
            col = local - row + lax.bitwise_and(row, 1)
            row = jnp.where(slot < count, row * BS, spare)
            row = pl.multiple_of(row, BS)
            col = pl.multiple_of(col * BS, BS)
            dense_ref[pl.ds(row, BS), pl.ds(col, BS)] = blocks[slot]
            return carry

        lax.fori_loop(i * each, (i + 1) * each, place, 0, unroll=True)


def assemble(block_values, rows, cols, count, stripe_rows):
    chunks = 4
    shape = (stripe_rows + BS, WIDTH)
    smem = pl.BlockSpec(memory_space=pltpu.SMEM)
    return pl.pallas_call(
        functools.partial(assemble_kernel, chunks),
        in_specs=[smem, smem, smem, pl.BlockSpec(memory_space=pltpu.HBM)],
        out_specs=whole(),
        out_shape=sds(shape, BF16),
        scratch_shapes=[
            pltpu.VMEM(block_values.shape, BF16),
            pltpu.SemaphoreType.DMA((chunks,)),
        ],
        compiler_params=params(24),
        name="assemble",
    )(in_hbm(rows), in_hbm(cols), count, in_hbm(block_values))


def in_hbm(value):
    return pltpu.with_memory_space_constraint(value, pltpu.HBM)


def tiles_of(stripe):
    return [(t, slice(t * TILE, (t + 1) * TILE)) for t in range(stripe // TILE)]


def on_sides(near, body):
    odd = lax.bitwise_and(lax.axis_index("x"), 1) == 1
    to_left = odd if near else jnp.logical_not(odd)

    @pl.when(to_left)
    def _():
        body(left_product)

    @pl.when(jnp.logical_not(to_left))
    def _():
        body(right_product)


def left_product(dense, piece, t, at):
    return dot(dense[at, : piece.shape[1] - t * TILE], piece[:, t * TILE :], NT)


def right_product(dense, piece, t, at):
    start = 2 * piece.shape[1] - t * TILE
    return dot(dense[at, start:], piece[:, : (t + 1) * TILE], NT)


def own_product(dense, piece, t, at):
    start = piece.shape[1] - t * TILE
    return dot(dense[at, start : start + piece.shape[1]], piece[...], NT)


def near_kernel(own, near, dense, acc):
    def body(product):
        for t, at in tiles_of(own.shape[1]):
            acc[at, :] = own_product(dense, own, t, at) + product(dense, near, t, at)

    on_sides(True, body)


def prop_in_kernel(far, acc, labels, dense, out):
    channels = far.shape[0]
    tag = jnp.broadcast_to(labels[...].astype(F32), (TAG, labels.shape[1])).astype(BF16)
    for t, at in tiles_of(far.shape[1]):
        out[channels:, at] = tag if t == 0 else jnp.zeros_like(tag)

    def body(product):
        for t, at in tiles_of(far.shape[1]):
            total = acc[at, :] + product(dense, far, t, at)
            out[:channels, at] = total.T.astype(BF16)

    on_sides(False, body)


def prop_kernel(far, acc, dense, out):
    def body(product):
        for t, at in tiles_of(far.shape[1]):
            total = acc[at, :] + product(dense, far, t, at)
            out[:, at] = total.T.astype(BF16)

    on_sides(False, body)


def hidden_kernel(first, second, third, fourth, w_in, hidden, pre_own, prop_in, labels):
    yl = lax.axis_index("yl")
    co = lax.axis_index("co")
    hid = hidden.shape[0]
    half = hid // 2
    depth = prop_in.shape[0] // 4
    for part, dy, dc in ((first, 0, 0), (second, 0, 1), (third, 1, 0), (fourth, 1, 1)):
        place = (yl + dy - 2 * yl * dy) * 2 + (co + dc - 2 * co * dc)
        rows = pl.ds(pl.multiple_of(place * depth, depth), depth)
        prop_in[rows, :] = part[:depth, :]
        labels[:, pl.ds(pl.multiple_of(place * TILE, TILE), TILE)] = part[
            depth : depth + TAG, :TILE
        ].astype(F32)
    weight = w_in[:, pl.ds(pl.multiple_of(co * hid, hid), hid)]
    pre = dot(weight, prop_in[...], TN)
    inner = GELU_A * (pre + GELU_B * (pre * pre * pre))
    hidden[...] = (pre * (0.5 * (1.0 + jnp.tanh(inner)))).astype(BF16)
    pre_own[...] = jnp.where(yl == 0, pre[:half], pre[half:])


def logits_kernel(scale, own, other, w_out, labels, out, dl, share, scores):
    yl = lax.axis_index("yl")
    co = lax.axis_index("co")
    hid = own.shape[0]
    w_own = w_out[pl.ds(pl.multiple_of(co * hid, hid), hid), :]
    w_other = w_out[pl.ds(pl.multiple_of((1 - co) * hid, hid), hid), :]
    logit = dot(w_own, own[...], TN) + dot(w_other, other[...], TN)
    scores[...] = logit
    start = pl.multiple_of((yl * 2 + co) * out.shape[1], out.shape[1])
    out[...] = scores[:, pl.ds(start, out.shape[1])]
    shifted = logit - jnp.max(logit, axis=0, keepdims=True)
    exponent = jnp.exp(shifted)
    probability = exponent / jnp.sum(exponent, axis=0, keepdims=True)
    classes = lax.broadcasted_iota(jnp.int32, logit.shape, 0).astype(F32)
    onehot = jnp.where(classes == labels[0:1, :], 1.0, 0.0)
    dlogits = ((probability - onehot) * scale).astype(BF16)
    dl[...] = dlogits
    rows = share.shape[0]
    mine = own[pl.ds(pl.multiple_of(yl * rows, rows), rows), :]
    share[...] = dot(mine, dlogits, NT)


def grads_kernel(far, acc, w_out, pre_own, prop_in, share_out, dense, out, total):
    def body(product):
        for t, at in tiles_of(far.shape[1]):
            total[at, :] = acc[at, :] + product(dense, far, t, at)

    on_sides(False, body)
    yl = lax.axis_index("yl")
    co = lax.axis_index("co")
    half = pre_own.shape[0]
    w = w_out[pl.ds(pl.multiple_of((co * 2 + yl) * half, half), half), :]
    share = None
    for t, at in tiles_of(far.shape[1]):
        spread = total[at, :]
        high = spread.astype(BF16)
        rest = spread - high.astype(F32)
        middle = rest.astype(BF16)
        low = (rest - middle.astype(F32)).astype(BF16)
        back = dot(w, high, NT) + (dot(w, middle, NT) + dot(w, low, NT))
        v = pre_own[:, at]
        th = jnp.tanh(GELU_A * (v + GELU_B * (v * v * v)))
        slope = 0.5 * (1.0 + th) + (0.5 * v) * (1.0 - th * th) * (
            GELU_A * (1.0 + (3.0 * GELU_B) * (v * v))
        )
        part = dot((back * slope).astype(BF16), prop_in[:, at], NT)
        share = part if share is None else share + part
    pieces, rows, _ = out.shape
    width = share.shape[1]
    for p in range(pieces):
        out[p, :, :width] = share[p * rows : (p + 1) * rows]
        out[p, :, width:] = share_out[p * rows : (p + 1) * rows]


def sum_kernel(parts, out):
    total = parts[0]
    for p in range(1, parts.shape[0]):
        total = total + parts[p]
    for p in range(out.shape[0]):
        out[p] = total


def collect_kernel(parts, grad_in, grad_out, rows_ref):
    planes = parts.shape[0] // 4
    rows = parts.shape[1]
    width = grad_in.shape[0]
    for p in range(planes):
        for yl in range(2):
            for co in range(2):
                at = ((co * 2 + yl) * planes + p) * rows
                rows_ref[at : at + rows, :] = parts[p * 4 + yl * 2 + co]
    grad_in[...] = rows_ref[:, :width].T
    grad_out[...] = rows_ref[:, width:]


def call(kernel, args, out_shape, mib=16, scratch=()):
    many = isinstance(out_shape, (tuple, list))
    return pl.pallas_call(
        kernel,
        in_specs=[whole()] * len(args),
        out_specs=[whole()] * len(out_shape) if many else whole(),
        out_shape=out_shape,
        scratch_shapes=list(scratch),
        compiler_params=params(mib),
    )(*args)


def halo(value):
    count = lax.axis_size(BLK)
    far = [(i, (i + 1 if i % 2 else i - 1) % count) for i in range(count)]
    far = lax.ppermute(value, BLK, far)
    near = lax.ppermute(value, BLK, [(i, i ^ 1) for i in range(count)])
    return near, far


def near_part(value, near, dense):
    shape = (value.shape[1], value.shape[0])
    return call(near_kernel, (value, near, dense), sds(shape, F32))


def flipped(value, axes):
    shift = {("co",): 1, ("yl",): 2, ("yl", "co"): 3}[axes]
    return lax.ppermute(value, FEAT, [(i, i ^ shift) for i in range(4)])


def on_device(
    features, block_values, block_rows, block_cols, block_count, labels, weight_in, weight_out
):
    devices = lax.axis_size(BLK)
    depth, stripe = features.shape
    node_scale = 1.0 / math.sqrt(devices * stripe)
    hid = weight_in.shape[1]
    classes = weight_out.shape[1]
    mine = labels.shape[0]

    near, far = halo(features)
    dense = assemble(block_values, block_rows, block_cols, block_count, stripe)
    first = call(
        prop_in_kernel,
        (far, near_part(features, near, dense), labels.reshape(1, mine), dense),
        sds((depth + TAG, stripe), BF16),
    )
    fourth = flipped(first, ("yl", "co"))
    third = flipped(first, ("yl",))
    second = flipped(first, ("co",))
    hidden, pre_own, prop_in, label_rows = call(
        hidden_kernel,
        (first, second, third, fourth, weight_in),
        (
            sds((hid // 2, stripe), BF16),
            sds((hid // 4, stripe), F32),
            sds((4 * depth, stripe), BF16),
            sds((8, stripe), F32),
        ),
    )

    near, far = halo(hidden)
    prop_own = call(
        prop_kernel, (far, near_part(hidden, near, dense), dense), sds((hid // 2, stripe), BF16)
    )
    prop_other = flipped(prop_own, ("co",))
    logits, dl, share_out = call(
        functools.partial(logits_kernel, node_scale),
        (prop_own, prop_other, weight_out, label_rows),
        (
            sds((classes, mine), F32),
            sds((classes, stripe), BF16),
            sds((hid // 4, classes), F32),
        ),
        scratch=[pltpu.VMEM((classes, stripe), F32)],
    )

    plane = lax.axis_size(PLANE)
    rows = hid // 4 // plane
    width = 4 * depth + classes
    near, far = halo(dl)
    share = call(
        grads_kernel,
        (
            far,
            near_part(dl, near, dense),
            weight_out,
            pre_own,
            prop_in,
            share_out,
            dense,
        ),
        sds((plane, rows, width), F32),
        scratch=[pltpu.VMEM((stripe, classes), F32)],
    )
    parts = lax.all_to_all(share, PLANE, 0, 0, tiled=True)
    parts = call(sum_kernel, (parts,), sds((lax.axis_size("z"), rows, width), F32))
    parts = lax.all_to_all(parts, "z", 0, 0, tiled=True)
    parts = call(sum_kernel, (parts,), sds((plane * 4, rows, width), F32))
    parts = lax.all_to_all(parts, PLANE + FEAT, 0, 0, tiled=True)
    grad_in, grad_out = call(
        collect_kernel,
        (parts,),
        (sds((4 * depth, hid), F32), sds((hid, classes), F32)),
        scratch=[pltpu.VMEM((hid, width), F32)],
    )
    return (logits, grad_in, grad_out)


def solution(mesh):
    fine = Mesh(mesh.devices.reshape(2, 16, 4, 2, 2), BLK + FEAT)
    placed = (
        P(FEAT, BLK),
        P(BLK, None, None),
        P(BLK),
        P(BLK),
        P(BLK),
        P(BLK + FEAT),
        P(),
        P(),
    )
    return jax.shard_map(
        on_device,
        mesh=fine,
        in_specs=placed,
        out_specs=(P(None, BLK + FEAT), P(), P()),
        check_vma=False,
    )
```

```python
import functools
import math

import jax
import jax.numpy as jnp
from jax import lax
from jax.experimental import pallas as pl
from jax.experimental.pallas import tpu as pltpu
from jax.sharding import Mesh
from jax.sharding import PartitionSpec as P


BLK = ("yh", "z", "x")
FEAT = ("yl", "co")
PLANE = ("yh", "x")
F32 = jnp.float32
BF16 = jnp.bfloat16
BS = 128
WIDTH = 18 * BS
TILE = 2 * BS
TAG = 8
NT = (((1,), (1,)), ((), ()))
NN = (((1,), (0,)), ((), ()))
TN = (((0,), (0,)), ((), ()))
GELU_A = math.sqrt(2.0 / math.pi)
GELU_B = 0.044715


def dot(a, b, dims):
    return lax.dot_general(a, b, dims, preferred_element_type=F32)


def params(mib):
    return pltpu.CompilerParams(vmem_limit_bytes=mib << 20)


def whole():
    return pl.BlockSpec(memory_space=pltpu.VMEM)


def sds(shape, dtype):
    return jax.ShapeDtypeStruct(shape, dtype)


def assemble_kernel(chunks, rows_ref, cols_ref, count_ref, blocks_hbm, dense_ref, blocks, sems):
    slots = blocks.shape[0]
    each = slots // chunks
    copies = [
        pltpu.make_async_copy(
            blocks_hbm.at[pl.ds(i * each, each)], blocks.at[pl.ds(i * each, each)], sems.at[i]
        )
        for i in range(chunks)
    ]
    for copy in copies:
        copy.start()
    spare = dense_ref.shape[0] - BS
    total_blocks = spare // BS * lax.axis_size(BLK)
    first = (lax.axis_index(BLK) - 1) * (spare // BS)
    count = count_ref[0]
    dense_ref[...] = jnp.zeros_like(dense_ref)
    for i in range(chunks):
        copies[i].wait()

        def place(slot, carry):
            row = rows_ref[slot]
            local = cols_ref[slot] - first
            local = jnp.where(local < 0, local + total_blocks, local)
            local = jnp.where(local >= total_blocks, local - total_blocks, local)
            col = local - row + lax.bitwise_and(row, 1)
            row = jnp.where(slot < count, row * BS, spare)
            row = pl.multiple_of(row, BS)
            col = pl.multiple_of(col * BS, BS)
            dense_ref[pl.ds(row, BS), pl.ds(col, BS)] = blocks[slot]
            return carry

        lax.fori_loop(i * each, (i + 1) * each, place, 0, unroll=True)


def assemble(block_values, rows, cols, count, stripe_rows):
    chunks = 4
    shape = (stripe_rows + BS, WIDTH)
    smem = pl.BlockSpec(memory_space=pltpu.SMEM)
    return pl.pallas_call(
        functools.partial(assemble_kernel, chunks),
        in_specs=[smem, smem, smem, pl.BlockSpec(memory_space=pltpu.HBM)],
        out_specs=whole(),
        out_shape=sds(shape, BF16),
        scratch_shapes=[
            pltpu.VMEM(block_values.shape, BF16),
            pltpu.SemaphoreType.DMA((chunks,)),
        ],
        compiler_params=params(24),
        name="assemble",
    )(in_hbm(rows), in_hbm(cols), count, in_hbm(block_values))


def in_hbm(value):
    return pltpu.with_memory_space_constraint(value, pltpu.HBM)


def tiles_of(stripe):
    return [(t, slice(t * TILE, (t + 1) * TILE)) for t in range(stripe // TILE)]


def on_sides(near, body):
    odd = lax.bitwise_and(lax.axis_index("x"), 1) == 1
    to_left = odd if near else jnp.logical_not(odd)

    @pl.when(to_left)
    def _():
        body(left_product)

    @pl.when(jnp.logical_not(to_left))
    def _():
        body(right_product)


def left_product(dense, piece, t, at):
    return dot(dense[at, : piece.shape[1] - t * TILE], piece[:, t * TILE :], NT)


def right_product(dense, piece, t, at):
    start = 2 * piece.shape[1] - t * TILE
    return dot(dense[at, start:], piece[:, : (t + 1) * TILE], NT)


def own_product(dense, piece, t, at):
    start = piece.shape[1] - t * TILE
    return dot(dense[at, start : start + piece.shape[1]], piece[...], NT)


def start_kernel(near, own, piece, dense, acc):
    def body(product):
        for t, at in tiles_of(own.shape[1]):
            acc[at, :] = own_product(dense, own, t, at) + product(dense, piece, t, at)

    on_sides(near, body)


def prop_in_kernel(far, acc, labels, dense, out):
    channels = far.shape[0]
    tag = jnp.broadcast_to(labels[...].astype(F32), (TAG, labels.shape[1])).astype(BF16)
    for t, at in tiles_of(far.shape[1]):
        out[channels:, at] = tag if t == 0 else jnp.zeros_like(tag)

    def body(product):
        for t, at in tiles_of(far.shape[1]):
            total = acc[at, :] + product(dense, far, t, at)
            out[:channels, at] = total.T.astype(BF16)

    on_sides(False, body)


def gather_kernel(first, second, third, fourth, prop_in, half, labels):
    yl = lax.axis_index("yl")
    co = lax.axis_index("co")
    depth = prop_in.shape[0] // 4
    for part, dy, dc in ((first, 0, 0), (second, 0, 1), (third, 1, 0), (fourth, 1, 1)):
        place = (yl + dy - 2 * yl * dy) * 2 + (co + dc - 2 * co * dc)
        rows = pl.ds(pl.multiple_of(place * depth, depth), depth)
        prop_in[rows, :] = part[:depth, :]
        labels[:, pl.ds(pl.multiple_of(place * TILE, TILE), TILE)] = part[
            depth : depth + TAG, :TILE
        ].astype(F32)
    rows = half.shape[0]
    half[...] = prop_in[pl.ds(pl.multiple_of(co * rows, rows), rows), :]


def hidden_of(prop_in, w_in, hidden, pre_part):
    yl = lax.axis_index("yl")
    co = lax.axis_index("co")
    hid = hidden.shape[0]
    weight = w_in[:, pl.ds(pl.multiple_of(co * hid, hid), hid)]
    pre = dot(weight, prop_in[...], TN)
    inner = GELU_A * (pre + GELU_B * (pre * pre * pre))
    hidden[...] = (pre * (0.5 * (1.0 + jnp.tanh(inner)))).astype(BF16)
    pre_part[...] = jnp.where(yl == 0, pre[: hid // 2], pre[hid // 2 :])


def own_hidden_kernel(prop_in, w_in, dense, acc, pre_part, hidden):
    hidden_of(prop_in, w_in, hidden, pre_part)
    for t, at in tiles_of(hidden.shape[1]):
        acc[at, :] = own_product(dense, hidden, t, at)


def join_halves(mine, other, out):
    co = lax.axis_index("co")
    half = mine.shape[0]
    out[pl.ds(pl.multiple_of(co * half, half), half), :] = mine[...]
    out[pl.ds(pl.multiple_of((1 - co) * half, half), half), :] = other[...]


def prop_hidden_kernel(
    near, near_other, far, far_other, w_in, acc, dense,
    out, near_in, far_in, pre_near, pre_far,
    hidden, total,
):
    join_halves(near, near_other, near_in)
    hidden_of(near_in, w_in, hidden, pre_near)

    def add_near(product):
        for t, at in tiles_of(out.shape[1]):
            total[at, :] = acc[at, :] + product(dense, hidden, t, at)

    on_sides(True, add_near)
    join_halves(far, far_other, far_in)
    hidden_of(far_in, w_in, hidden, pre_far)

    def add_far(product):
        for t, at in tiles_of(out.shape[1]):
            out[:, at] = (total[at, :] + product(dense, hidden, t, at)).T.astype(BF16)

    on_sides(False, add_far)


def logits_kernel(scale, own, other, w_out, labels, out, dl, share, scores):
    yl = lax.axis_index("yl")
    co = lax.axis_index("co")
    hid = own.shape[0]
    w_own = w_out[pl.ds(pl.multiple_of(co * hid, hid), hid), :]
    w_other = w_out[pl.ds(pl.multiple_of((1 - co) * hid, hid), hid), :]
    logit = dot(w_own, own[...], TN) + dot(w_other, other[...], TN)
    scores[...] = logit
    start = pl.multiple_of((yl * 2 + co) * out.shape[1], out.shape[1])
    out[...] = scores[:, pl.ds(start, out.shape[1])]
    shifted = logit - jnp.max(logit, axis=0, keepdims=True)
    exponent = jnp.exp(shifted)
    probability = exponent / jnp.sum(exponent, axis=0, keepdims=True)
    classes = lax.broadcasted_iota(jnp.int32, logit.shape, 0).astype(F32)
    onehot = jnp.where(classes == labels[0:1, :], 1.0, 0.0)
    dlogits = ((probability - onehot) * scale).astype(BF16)
    dl[...] = dlogits
    rows = share.shape[0]
    mine = own[pl.ds(pl.multiple_of(yl * rows, rows), rows), :]
    share[...] = dot(mine, dlogits, NT)


def grads_kernel(
    dl, dense, w_out, pre_own, pre_near, pre_far, own_in, near_in, far_in, share_out, out
):
    odd = lax.bitwise_and(lax.axis_index("x"), 1) == 1
    yl = lax.axis_index("yl")
    co = lax.axis_index("co")
    half = pre_own.shape[0]
    w = w_out[pl.ds(pl.multiple_of((co * 2 + yl) * half, half), half), :]
    tiles = tiles_of(dl.shape[1])
    reach = dense.shape[1] // TILE
    share = None
    for block in range(3 * len(tiles)):
        spread = None
        for t, at in tiles:
            if 0 <= block - t < reach:
                part = dot(dl[:, at], dense[at, (block - t) * TILE : (block - t + 1) * TILE], NN)
                spread = part if spread is None else spread + part
        high = spread.astype(BF16)
        rest = spread - high.astype(F32)
        middle = rest.astype(BF16)
        low = (rest - middle.astype(F32)).astype(BF16)
        back = dot(w, high, NN) + (dot(w, middle, NN) + dot(w, low, NN))
        stripe, tile = divmod(block, len(tiles))
        at = tiles[tile][1]
        if stripe == 1:
            v, prop_in = pre_own[:, at], own_in[:, at]
        else:
            is_near = odd if stripe == 0 else jnp.logical_not(odd)
            v = jnp.where(is_near, pre_near[:, at], pre_far[:, at])
            prop_in = jnp.where(is_near, near_in[:, at], far_in[:, at])
        th = jnp.tanh(GELU_A * (v + GELU_B * (v * v * v)))
        slope = 0.5 * (1.0 + th) + (0.5 * v) * (1.0 - th * th) * (
            GELU_A * (1.0 + (3.0 * GELU_B) * (v * v))
        )
        grad = back * slope
        high = grad.astype(BF16)
        low = (grad - high.astype(F32)).astype(BF16)
        part = dot(high, prop_in, NT) + dot(low, prop_in, NT)
        share = part if share is None else share + part
    pieces, rows, _ = out.shape
    width = share.shape[1]
    for p in range(pieces):
        out[p, :, :width] = share[p * rows : (p + 1) * rows]
        out[p, :, width:] = share_out[p * rows : (p + 1) * rows]


def sum_kernel(parts, out):
    total = parts[0]
    for p in range(1, parts.shape[0]):
        total = total + parts[p]
    for p in range(out.shape[0]):
        out[p] = total


def collect_kernel(parts, grad_in, grad_out, rows_ref):
    planes = parts.shape[0] // 4
    rows = parts.shape[1]
    width = grad_in.shape[0]
    for p in range(planes):
        for yl in range(2):
            for co in range(2):
                at = ((co * 2 + yl) * planes + p) * rows
                rows_ref[at : at + rows, :] = parts[p * 4 + yl * 2 + co]
    grad_in[...] = rows_ref[:, :width].T
    grad_out[...] = rows_ref[:, width:]


def call(kernel, args, out_shape, mib=16, scratch=()):
    many = isinstance(out_shape, (tuple, list))
    return pl.pallas_call(
        kernel,
        in_specs=[whole()] * len(args),
        out_specs=[whole()] * len(out_shape) if many else whole(),
        out_shape=out_shape,
        scratch_shapes=list(scratch),
        compiler_params=params(mib),
    )(*args)


def halo(value):
    count = lax.axis_size(BLK)
    far = [(i, (i + 1 if i % 2 else i - 1) % count) for i in range(count)]
    far = lax.ppermute(value, BLK, far)
    near = lax.ppermute(value, BLK, [(i, i ^ 1) for i in range(count)])
    return near, far


def start_part(own, piece, dense, near):
    shape = (own.shape[1], own.shape[0])
    return call(functools.partial(start_kernel, near), (own, piece, dense), sds(shape, F32))


def flipped(value, axes):
    shift = {("co",): 1, ("yl",): 2}[axes]
    return lax.ppermute(value, FEAT, [(i, i ^ shift) for i in range(4)])


def on_device(
    features, block_values, block_rows, block_cols, block_count, labels, weight_in, weight_out
):
    devices = lax.axis_size(BLK)
    depth, stripe = features.shape
    node_scale = 1.0 / math.sqrt(devices * stripe)
    hid = weight_in.shape[1]
    classes = weight_out.shape[1]
    mine = labels.shape[0]

    near, far = halo(features)
    dense = assemble(block_values, block_rows, block_cols, block_count, stripe)
    first = call(
        prop_in_kernel,
        (far, start_part(features, near, dense, True), labels.reshape(1, mine), dense),
        sds((depth + TAG, stripe), BF16),
    )
    third = flipped(first, ("yl",))
    second = flipped(first, ("co",))
    fourth = flipped(third, ("co",))
    half_rows = 2 * depth
    prop_in, half_in, label_rows = call(
        gather_kernel,
        (first, second, third, fourth),
        (
            sds((4 * depth, stripe), BF16),
            sds((half_rows, stripe), BF16),
            sds((TAG, stripe), F32),
        ),
    )
    near, far = halo(half_in)
    pre = sds((hid // 4, stripe), F32)
    hidden = pltpu.VMEM((hid // 2, stripe), BF16)
    acc, pre_own = call(
        own_hidden_kernel,
        (prop_in, weight_in, dense),
        (sds((stripe, hid // 2), F32), pre),
        scratch=[hidden],
    )
    whole_in = sds((4 * depth, stripe), BF16)
    prop_own, near_in, far_in, pre_near, pre_far = call(
        prop_hidden_kernel,
        (near, flipped(near, ("co",)), far, flipped(far, ("co",)), weight_in, acc, dense),
        (sds((hid // 2, stripe), BF16), whole_in, whole_in, pre, pre),
        scratch=[hidden, pltpu.VMEM((stripe, hid // 2), F32)],
    )
    prop_other = flipped(prop_own, ("co",))
    logits, dl, share_out = call(
        functools.partial(logits_kernel, node_scale),
        (prop_own, prop_other, weight_out, label_rows),
        (
            sds((classes, mine), F32),
            sds((classes, stripe), BF16),
            sds((hid // 4, classes), F32),
        ),
        scratch=[pltpu.VMEM((classes, stripe), F32)],
    )

    plane = lax.axis_size(PLANE)
    rows = hid // 4 // plane
    width = 4 * depth + classes
    share = call(
        grads_kernel,
        (
            dl,
            dense,
            weight_out,
            pre_own,
            pre_near,
            pre_far,
            prop_in,
            near_in,
            far_in,
            share_out,
        ),
        sds((plane, rows, width), F32),
    )
    parts = lax.all_to_all(share, PLANE, 0, 0, tiled=True)
    parts = call(sum_kernel, (parts,), sds((lax.axis_size("z"), rows, width), F32))
    parts = lax.all_to_all(parts, "z", 0, 0, tiled=True)
    parts = call(sum_kernel, (parts,), sds((plane * 4, rows, width), F32))
    parts = lax.all_to_all(parts, PLANE + FEAT, 0, 0, tiled=True)
    grad_in, grad_out = call(
        collect_kernel,
        (parts,),
        (sds((4 * depth, hid), F32), sds((hid, classes), F32)),
        scratch=[pltpu.VMEM((hid, width), F32)],
    )
    return (logits, grad_in, grad_out)


def solution(mesh):
    fine = Mesh(mesh.devices.reshape(2, 16, 4, 2, 2), BLK + FEAT)
    placed = (
        P(FEAT, BLK),
        P(BLK, None, None),
        P(BLK),
        P(BLK),
        P(BLK),
        P(BLK + FEAT),
        P(),
        P(),
    )
    return jax.shard_map(
        on_device,
        mesh=fine,
        in_specs=placed,
        out_specs=(P(None, BLK + FEAT), P(), P()),
        check_vma=False,
    )
```

```python
import functools
import math

import jax
import jax.numpy as jnp
from jax import lax
from jax.experimental import pallas as pl
from jax.experimental.pallas import tpu as pltpu
from jax.sharding import Mesh
from jax.sharding import PartitionSpec as P


BLK = ("yh", "z", "x")
FEAT = ("yl", "co")
PLANE = ("yh", "x")
F32 = jnp.float32
BF16 = jnp.bfloat16
BS = 128
WIDTH = 18 * BS
TILE = 2 * BS
TAG = 8
NT = (((1,), (1,)), ((), ()))
NN = (((1,), (0,)), ((), ()))
TN = (((0,), (0,)), ((), ()))
GELU_A = math.sqrt(2.0 / math.pi)
GELU_B = 0.044715


def dot(a, b, dims):
    return lax.dot_general(a, b, dims, preferred_element_type=F32)


def params(mib):
    return pltpu.CompilerParams(vmem_limit_bytes=mib << 20)


def whole():
    return pl.BlockSpec(memory_space=pltpu.VMEM)


def sds(shape, dtype):
    return jax.ShapeDtypeStruct(shape, dtype)


def assemble_kernel(chunks, rows_ref, cols_ref, count_ref, blocks_hbm, dense_ref, blocks, sems):
    slots = blocks.shape[0]
    each = slots // chunks
    copies = [
        pltpu.make_async_copy(
            blocks_hbm.at[pl.ds(i * each, each)], blocks.at[pl.ds(i * each, each)], sems.at[i]
        )
        for i in range(chunks)
    ]
    for copy in copies:
        copy.start()
    spare = dense_ref.shape[0] - BS
    total_blocks = spare // BS * lax.axis_size(BLK)
    first = (lax.axis_index(BLK) - 1) * (spare // BS)
    count = count_ref[0]
    dense_ref[...] = jnp.zeros_like(dense_ref)
    for i in range(chunks):
        copies[i].wait()

        def place(slot, carry):
            row = rows_ref[slot]
            local = cols_ref[slot] - first
            local = jnp.where(local < 0, local + total_blocks, local)
            local = jnp.where(local >= total_blocks, local - total_blocks, local)
            col = local - row + lax.bitwise_and(row, 1)
            row = jnp.where(slot < count, row * BS, spare)
            row = pl.multiple_of(row, BS)
            col = pl.multiple_of(col * BS, BS)
            dense_ref[pl.ds(row, BS), pl.ds(col, BS)] = blocks[slot]
            return carry

        lax.fori_loop(i * each, (i + 1) * each, place, 0, unroll=True)


def assemble(block_values, rows, cols, count, stripe_rows):
    chunks = 4
    shape = (stripe_rows + BS, WIDTH)
    smem = pl.BlockSpec(memory_space=pltpu.SMEM)
    return pl.pallas_call(
        functools.partial(assemble_kernel, chunks),
        in_specs=[smem, smem, smem, pl.BlockSpec(memory_space=pltpu.HBM)],
        out_specs=whole(),
        out_shape=sds(shape, BF16),
        scratch_shapes=[
            pltpu.VMEM(block_values.shape, BF16),
            pltpu.SemaphoreType.DMA((chunks,)),
        ],
        compiler_params=params(24),
        name="assemble",
    )(in_hbm(rows), in_hbm(cols), count, in_hbm(block_values))


def in_hbm(value):
    return pltpu.with_memory_space_constraint(value, pltpu.HBM)


def tiles_of(stripe):
    return [(t, slice(t * TILE, (t + 1) * TILE)) for t in range(stripe // TILE)]


def on_sides(near, body):
    odd = lax.bitwise_and(lax.axis_index("x"), 1) == 1
    to_left = odd if near else jnp.logical_not(odd)

    @pl.when(to_left)
    def _():
        body(left_product)

    @pl.when(jnp.logical_not(to_left))
    def _():
        body(right_product)


def left_product(dense, piece, t, at):
    return dot(dense[at, : piece.shape[1] - t * TILE], piece[:, t * TILE :], NT)


def right_product(dense, piece, t, at):
    start = 2 * piece.shape[1] - t * TILE
    return dot(dense[at, start:], piece[:, : (t + 1) * TILE], NT)


def own_product(dense, piece, t, at):
    start = piece.shape[1] - t * TILE
    return dot(dense[at, start : start + piece.shape[1]], piece[...], NT)


def start_kernel(near, own, piece, dense, acc):
    def body(product):
        for t, at in tiles_of(own.shape[1]):
            acc[at, :] = own_product(dense, own, t, at) + product(dense, piece, t, at)

    on_sides(near, body)


def prop_in_kernel(far, acc, labels, dense, out, plain):
    channels = far.shape[0]
    tag = jnp.broadcast_to(labels[...].astype(F32), (TAG, labels.shape[1])).astype(BF16)
    for t, at in tiles_of(far.shape[1]):
        out[channels:, at] = tag if t == 0 else jnp.zeros_like(tag)

    def body(product):
        for t, at in tiles_of(far.shape[1]):
            total = acc[at, :] + product(dense, far, t, at)
            value = total.T.astype(BF16)
            out[:channels, at] = value
            plain[:, at] = value

    on_sides(False, body)


def stack_kernel(near, far, both):
    rows = near.shape[0]
    both[:rows, :] = near[...]
    both[rows:, :] = far[...]


def gather(parts, place_part):
    yl = lax.axis_index("yl")
    co = lax.axis_index("co")
    for part, (dy, dc) in zip(parts, ((0, 0), (0, 1), (1, 0), (1, 1))):
        place_part(part, (yl + dy - 2 * yl * dy) * 2 + (co + dc - 2 * co * dc))


def hidden_of(prop_in, w_in, hidden, pre_part):
    yl = lax.axis_index("yl")
    co = lax.axis_index("co")
    hid = hidden.shape[0]
    weight = w_in[:, pl.ds(pl.multiple_of(co * hid, hid), hid)]
    pre = dot(weight, prop_in[...], TN)
    inner = GELU_A * (pre + GELU_B * (pre * pre * pre))
    hidden[...] = (pre * (0.5 * (1.0 + jnp.tanh(inner)))).astype(BF16)
    pre_part[...] = jnp.where(yl == 0, pre[: hid // 2], pre[hid // 2 :])


def own_hidden_kernel(
    first, second, third, fourth, w_in, dense, acc, pre_part, prop_in, labels, hidden
):
    depth = prop_in.shape[0] // 4

    def place_part(part, place):
        prop_in[pl.ds(pl.multiple_of(place * depth, depth), depth), :] = part[:depth, :]
        labels[:, pl.ds(pl.multiple_of(place * TILE, TILE), TILE)] = part[
            depth : depth + TAG, :TILE
        ].astype(F32)

    gather((first, second, third, fourth), place_part)
    hidden_of(prop_in, w_in, hidden, pre_part)
    for t, at in tiles_of(hidden.shape[1]):
        acc[at, :] = own_product(dense, hidden, t, at)


def prop_hidden_kernel(
    first, second, third, fourth, w_in, acc, dense,
    out, near_in, far_in, pre_near, pre_far,
    hidden, total,
):
    depth = near_in.shape[0] // 4

    def place_part(part, place):
        rows = pl.ds(pl.multiple_of(place * depth, depth), depth)
        near_in[rows, :] = part[:depth, :]
        far_in[rows, :] = part[depth:, :]

    gather((first, second, third, fourth), place_part)
    hidden_of(near_in, w_in, hidden, pre_near)

    def add_near(product):
        for t, at in tiles_of(out.shape[1]):
            total[at, :] = acc[at, :] + product(dense, hidden, t, at)

    on_sides(True, add_near)
    hidden_of(far_in, w_in, hidden, pre_far)

    def add_far(product):
        for t, at in tiles_of(out.shape[1]):
            out[:, at] = (total[at, :] + product(dense, hidden, t, at)).T.astype(BF16)

    on_sides(False, add_far)


def logits_kernel(scale, own, other, w_out, labels, out, dl, share, scores):
    yl = lax.axis_index("yl")
    co = lax.axis_index("co")
    hid = own.shape[0]
    w_own = w_out[pl.ds(pl.multiple_of(co * hid, hid), hid), :]
    w_other = w_out[pl.ds(pl.multiple_of((1 - co) * hid, hid), hid), :]
    logit = dot(w_own, own[...], TN) + dot(w_other, other[...], TN)
    scores[...] = logit
    start = pl.multiple_of((yl * 2 + co) * out.shape[1], out.shape[1])
    out[...] = scores[:, pl.ds(start, out.shape[1])]
    shifted = logit - jnp.max(logit, axis=0, keepdims=True)
    exponent = jnp.exp(shifted)
    probability = exponent / jnp.sum(exponent, axis=0, keepdims=True)
    classes = lax.broadcasted_iota(jnp.int32, logit.shape, 0).astype(F32)
    onehot = jnp.where(classes == labels[0:1, :], 1.0, 0.0)
    dlogits = ((probability - onehot) * scale).astype(BF16)
    dl[...] = dlogits
    rows = share.shape[0]
    mine = own[pl.ds(pl.multiple_of(yl * rows, rows), rows), :]
    share[...] = dot(mine, dlogits, NT)


def grads_kernel(
    dl, dense, w_out, pre_own, pre_near, pre_far, own_in, near_in, far_in, share_out, out
):
    odd = lax.bitwise_and(lax.axis_index("x"), 1) == 1
    yl = lax.axis_index("yl")
    co = lax.axis_index("co")
    half = pre_own.shape[0]
    w = w_out[pl.ds(pl.multiple_of((co * 2 + yl) * half, half), half), :]
    tiles = tiles_of(dl.shape[1])
    reach = dense.shape[1] // TILE
    share = None
    for block in range(3 * len(tiles)):
        spread = None
        for t, at in tiles:
            if 0 <= block - t < reach:
                part = dot(dl[:, at], dense[at, (block - t) * TILE : (block - t + 1) * TILE], NN)
                spread = part if spread is None else spread + part
        high = spread.astype(BF16)
        rest = spread - high.astype(F32)
        middle = rest.astype(BF16)
        low = (rest - middle.astype(F32)).astype(BF16)
        back = dot(w, high, NN) + (dot(w, middle, NN) + dot(w, low, NN))
        stripe, tile = divmod(block, len(tiles))
        at = tiles[tile][1]
        if stripe == 1:
            v, prop_in = pre_own[:, at], own_in[:, at]
        else:
            is_near = odd if stripe == 0 else jnp.logical_not(odd)
            v = jnp.where(is_near, pre_near[:, at], pre_far[:, at])
            prop_in = jnp.where(is_near, near_in[:, at], far_in[:, at])
        th = jnp.tanh(GELU_A * (v + GELU_B * (v * v * v)))
        slope = 0.5 * (1.0 + th) + (0.5 * v) * (1.0 - th * th) * (
            GELU_A * (1.0 + (3.0 * GELU_B) * (v * v))
        )
        grad = back * slope
        high = grad.astype(BF16)
        low = (grad - high.astype(F32)).astype(BF16)
        part = dot(high, prop_in, NT) + dot(low, prop_in, NT)
        share = part if share is None else share + part
    pieces, rows, _ = out.shape
    width = share.shape[1]
    for p in range(pieces):
        out[p, :, :width] = share[p * rows : (p + 1) * rows]
        out[p, :, width:] = share_out[p * rows : (p + 1) * rows]


def sum_kernel(parts, out):
    total = parts[0]
    for p in range(1, parts.shape[0]):
        total = total + parts[p]
    for p in range(out.shape[0]):
        out[p] = total


def collect_kernel(parts, grad_in, grad_out, rows_ref):
    planes = parts.shape[0] // 4
    rows = parts.shape[1]
    width = grad_in.shape[0]
    for p in range(planes):
        for yl in range(2):
            for co in range(2):
                at = ((co * 2 + yl) * planes + p) * rows
                rows_ref[at : at + rows, :] = parts[p * 4 + yl * 2 + co]
    grad_in[...] = rows_ref[:, :width].T
    grad_out[...] = rows_ref[:, width:]


def call(kernel, args, out_shape, mib=16, scratch=()):
    many = isinstance(out_shape, (tuple, list))
    return pl.pallas_call(
        kernel,
        in_specs=[whole()] * len(args),
        out_specs=[whole()] * len(out_shape) if many else whole(),
        out_shape=out_shape,
        scratch_shapes=list(scratch),
        compiler_params=params(mib),
    )(*args)


def halo(value):
    count = lax.axis_size(BLK)
    far = [(i, (i + 1 if i % 2 else i - 1) % count) for i in range(count)]
    far = lax.ppermute(value, BLK, far)
    near = lax.ppermute(value, BLK, [(i, i ^ 1) for i in range(count)])
    return near, far


def start_part(own, piece, dense, near):
    shape = (own.shape[1], own.shape[0])
    return call(functools.partial(start_kernel, near), (own, piece, dense), sds(shape, F32))


def flipped(value, axis):
    shift = {"co": 1, "yl": 2}[axis]
    return lax.ppermute(value, FEAT, [(i, i ^ shift) for i in range(4)])


def on_device(
    features, block_values, block_rows, block_cols, block_count, labels, weight_in, weight_out
):
    devices = lax.axis_size(BLK)
    depth, stripe = features.shape
    node_scale = 1.0 / math.sqrt(devices * stripe)
    hid = weight_in.shape[1]
    classes = weight_out.shape[1]
    mine = labels.shape[0]

    near, far = halo(features)
    dense = assemble(block_values, block_rows, block_cols, block_count, stripe)
    first, plain = call(
        prop_in_kernel,
        (far, start_part(features, near, dense, True), labels.reshape(1, mine), dense),
        (sds((depth + TAG, stripe), BF16), sds((depth, stripe), BF16)),
    )
    near, far = halo(plain)
    third = flipped(first, "yl")
    second = flipped(first, "co")
    fourth = flipped(third, "co")
    both = call(stack_kernel, (near, far), sds((2 * depth, stripe), BF16))
    both_third = flipped(both, "yl")
    both_second = flipped(both, "co")
    both_fourth = flipped(both_third, "co")

    pre = sds((hid // 4, stripe), F32)
    hidden = pltpu.VMEM((hid // 2, stripe), BF16)
    whole_in = sds((4 * depth, stripe), BF16)
    acc, pre_own, prop_in, label_rows = call(
        own_hidden_kernel,
        (first, second, third, fourth, weight_in, dense),
        (sds((stripe, hid // 2), F32), pre, whole_in, sds((TAG, stripe), F32)),
        scratch=[hidden],
    )
    prop_own, near_in, far_in, pre_near, pre_far = call(
        prop_hidden_kernel,
        (both, both_second, both_third, both_fourth, weight_in, acc, dense),
        (sds((hid // 2, stripe), BF16), whole_in, whole_in, pre, pre),
        scratch=[hidden, pltpu.VMEM((stripe, hid // 2), F32)],
    )
    prop_other = flipped(prop_own, "co")
    logits, dl, share_out = call(
        functools.partial(logits_kernel, node_scale),
        (prop_own, prop_other, weight_out, label_rows),
        (
            sds((classes, mine), F32),
            sds((classes, stripe), BF16),
            sds((hid // 4, classes), F32),
        ),
        scratch=[pltpu.VMEM((classes, stripe), F32)],
    )

    plane = lax.axis_size(PLANE)
    rows = hid // 4 // plane
    width = 4 * depth + classes
    share = call(
        grads_kernel,
        (
            dl,
            dense,
            weight_out,
            pre_own,
            pre_near,
            pre_far,
            prop_in,
            near_in,
            far_in,
            share_out,
        ),
        sds((plane, rows, width), F32),
    )
    parts = lax.all_to_all(share, PLANE, 0, 0, tiled=True)
    parts = call(sum_kernel, (parts,), sds((lax.axis_size("z"), rows, width), F32))
    parts = lax.all_to_all(parts, "z", 0, 0, tiled=True)
    parts = call(sum_kernel, (parts,), sds((plane * 4, rows, width), F32))
    parts = lax.all_to_all(parts, PLANE + FEAT, 0, 0, tiled=True)
    grad_in, grad_out = call(
        collect_kernel,
        (parts,),
        (sds((4 * depth, hid), F32), sds((hid, classes), F32)),
        scratch=[pltpu.VMEM((hid, width), F32)],
    )
    return (logits, grad_in, grad_out)


def solution(mesh):
    fine = Mesh(mesh.devices.reshape(2, 16, 4, 2, 2), BLK + FEAT)
    placed = (
        P(FEAT, BLK),
        P(BLK, None, None),
        P(BLK),
        P(BLK),
        P(BLK),
        P(BLK + FEAT),
        P(),
        P(),
    )
    return jax.shard_map(
        on_device,
        mesh=fine,
        in_specs=placed,
        out_specs=(P(None, BLK + FEAT), P(), P()),
        check_vma=False,
    )
```

```python
import functools
import math

import jax
import jax.numpy as jnp
from jax import lax
from jax.experimental import pallas as pl
from jax.experimental.pallas import tpu as pltpu
from jax.sharding import Mesh
from jax.sharding import PartitionSpec as P


BLK = ("yh", "z", "x")
FEAT = ("yl", "co")
PLANE = ("yh", "x")
F32 = jnp.float32
BF16 = jnp.bfloat16
BS = 128
WIDTH = 18 * BS
TILE = 2 * BS
TAG = 8
NT = (((1,), (1,)), ((), ()))
NN = (((1,), (0,)), ((), ()))
TN = (((0,), (0,)), ((), ()))
GELU_A = math.sqrt(2.0 / math.pi)
GELU_B = 0.044715


def dot(a, b, dims):
    return lax.dot_general(a, b, dims, preferred_element_type=F32)


def params(mib):
    return pltpu.CompilerParams(vmem_limit_bytes=mib << 20)


def whole():
    return pl.BlockSpec(memory_space=pltpu.VMEM)


def sds(shape, dtype):
    return jax.ShapeDtypeStruct(shape, dtype)


def assemble_kernel(chunks, rows_ref, cols_ref, count_ref, blocks_hbm, dense_ref, blocks, sems):
    slots = blocks.shape[0]
    each = slots // chunks
    copies = [
        pltpu.make_async_copy(
            blocks_hbm.at[pl.ds(i * each, each)], blocks.at[pl.ds(i * each, each)], sems.at[i]
        )
        for i in range(chunks)
    ]
    for copy in copies:
        copy.start()
    spare = dense_ref.shape[0] - BS
    total_blocks = spare // BS * lax.axis_size(BLK)
    first = (lax.axis_index(BLK) - 1) * (spare // BS)
    count = count_ref[0]
    dense_ref[...] = jnp.zeros_like(dense_ref)
    for i in range(chunks):
        copies[i].wait()

        def place(slot, carry):
            row = rows_ref[slot]
            local = cols_ref[slot] - first
            local = jnp.where(local < 0, local + total_blocks, local)
            local = jnp.where(local >= total_blocks, local - total_blocks, local)
            col = local - row + lax.bitwise_and(row, 1)
            row = jnp.where(slot < count, row * BS, spare)
            row = pl.multiple_of(row, BS)
            col = pl.multiple_of(col * BS, BS)
            dense_ref[pl.ds(row, BS), pl.ds(col, BS)] = blocks[slot]
            return carry

        lax.fori_loop(i * each, (i + 1) * each, place, 0, unroll=True)


def assemble(block_values, rows, cols, count, stripe_rows):
    chunks = 4
    shape = (stripe_rows + BS, WIDTH)
    smem = pl.BlockSpec(memory_space=pltpu.SMEM)
    return pl.pallas_call(
        functools.partial(assemble_kernel, chunks),
        in_specs=[smem, smem, smem, pl.BlockSpec(memory_space=pltpu.HBM)],
        out_specs=whole(),
        out_shape=sds(shape, BF16),
        scratch_shapes=[
            pltpu.VMEM(block_values.shape, BF16),
            pltpu.SemaphoreType.DMA((chunks,)),
        ],
        compiler_params=params(24),
        name="assemble",
    )(in_hbm(rows), in_hbm(cols), count, in_hbm(block_values))


def in_hbm(value):
    return pltpu.with_memory_space_constraint(value, pltpu.HBM)


def tiles_of(stripe):
    return [(t, slice(t * TILE, (t + 1) * TILE)) for t in range(stripe // TILE)]


def on_sides(near, body):
    odd = lax.bitwise_and(lax.axis_index("x"), 1) == 1
    to_left = odd if near else jnp.logical_not(odd)

    @pl.when(to_left)
    def _():
        body(left_product)

    @pl.when(jnp.logical_not(to_left))
    def _():
        body(right_product)


def left_product(dense, piece, t, at):
    return dot(dense[at, : piece.shape[1] - t * TILE], piece[:, t * TILE :], NT)


def right_product(dense, piece, t, at):
    start = 2 * piece.shape[1] - t * TILE
    return dot(dense[at, start:], piece[:, : (t + 1) * TILE], NT)


def own_product(dense, piece, t, at):
    start = piece.shape[1] - t * TILE
    return dot(dense[at, start : start + piece.shape[1]], piece[...], NT)


def start_kernel(near, own, piece, dense, acc):
    def body(product):
        for t, at in tiles_of(own.shape[1]):
            acc[at, :] = own_product(dense, own, t, at) + product(dense, piece, t, at)

    on_sides(near, body)


def prop_in_kernel(far, acc, labels, dense, out, plain):
    channels = far.shape[0]
    tag = jnp.broadcast_to(labels[...].astype(F32), (TAG, labels.shape[1])).astype(BF16)
    for t, at in tiles_of(far.shape[1]):
        out[channels:, at] = tag if t == 0 else jnp.zeros_like(tag)

    def body(product):
        for t, at in tiles_of(far.shape[1]):
            total = acc[at, :] + product(dense, far, t, at)
            value = total.T.astype(BF16)
            out[:channels, at] = value
            plain[:, at] = value

    on_sides(False, body)


def stack_kernel(near, far, both):
    rows = near.shape[0]
    both[:rows, :] = near[...]
    both[rows:, :] = far[...]


def gather(parts, place_part):
    yl = lax.axis_index("yl")
    co = lax.axis_index("co")
    for part, (dy, dc) in zip(parts, ((0, 0), (0, 1), (1, 0), (1, 1))):
        place_part(part, (yl + dy - 2 * yl * dy) * 2 + (co + dc - 2 * co * dc))


def hidden_of(prop_in, w_in, hidden, pre_part, whole_pre):
    yl = lax.axis_index("yl")
    co = lax.axis_index("co")
    pre = dot(w_in[...], prop_in[...], TN)
    inner = GELU_A * (pre + GELU_B * (pre * pre * pre))
    hidden[...] = (pre * (0.5 * (1.0 + jnp.tanh(inner)))).astype(BF16)
    whole_pre[...] = pre
    rows = pre_part.shape[0]
    pre_part[...] = whole_pre[pl.ds(pl.multiple_of((co * 2 + yl) * rows, rows), rows), :]


def own_hidden_kernel(
    first, second, third, fourth, w_in, dense, acc, pre_part, prop_in, labels, hidden, whole_pre
):
    depth = prop_in.shape[0] // 4

    def place_part(part, place):
        prop_in[pl.ds(pl.multiple_of(place * depth, depth), depth), :] = part[:depth, :]
        labels[:, pl.ds(pl.multiple_of(place * TILE, TILE), TILE)] = part[
            depth : depth + TAG, :TILE
        ].astype(F32)

    gather((first, second, third, fourth), place_part)
    hidden_of(prop_in, w_in, hidden, pre_part, whole_pre)
    for t, at in tiles_of(hidden.shape[1]):
        acc[at, :] = own_product(dense, hidden, t, at)


def prop_hidden_kernel(
    first, second, third, fourth, w_in, acc, dense,
    out, near_in, far_in, pre_near, pre_far,
    hidden, whole_pre, total,
):
    depth = near_in.shape[0] // 4

    def place_part(part, place):
        rows = pl.ds(pl.multiple_of(place * depth, depth), depth)
        near_in[rows, :] = part[:depth, :]
        far_in[rows, :] = part[depth:, :]

    gather((first, second, third, fourth), place_part)
    hidden_of(near_in, w_in, hidden, pre_near, whole_pre)

    def add_near(product):
        for t, at in tiles_of(out.shape[1]):
            total[at, :] = acc[at, :] + product(dense, hidden, t, at)

    on_sides(True, add_near)
    hidden_of(far_in, w_in, hidden, pre_far, whole_pre)

    def add_far(product):
        for t, at in tiles_of(out.shape[1]):
            out[:, at] = (total[at, :] + product(dense, hidden, t, at)).T.astype(BF16)

    on_sides(False, add_far)


def logits_kernel(scale, prop_hid, w_out, labels, out, dl, share, scores):
    yl = lax.axis_index("yl")
    co = lax.axis_index("co")
    logit = dot(w_out[...], prop_hid[...], TN)
    scores[...] = logit
    start = pl.multiple_of((yl * 2 + co) * out.shape[1], out.shape[1])
    out[...] = scores[:, pl.ds(start, out.shape[1])]
    shifted = logit - jnp.max(logit, axis=0, keepdims=True)
    exponent = jnp.exp(shifted)
    probability = exponent / jnp.sum(exponent, axis=0, keepdims=True)
    classes = lax.broadcasted_iota(jnp.int32, logit.shape, 0).astype(F32)
    onehot = jnp.where(classes == labels[0:1, :], 1.0, 0.0)
    dlogits = ((probability - onehot) * scale).astype(BF16)
    dl[...] = dlogits
    rows = share.shape[0]
    mine = prop_hid[pl.ds(pl.multiple_of((co * 2 + yl) * rows, rows), rows), :]
    share[...] = dot(mine, dlogits, NT)


def grads_kernel(
    dl, dense, w_out, pre_own, pre_near, pre_far, own_in, near_in, far_in, share_out, out, terms
):
    odd = lax.bitwise_and(lax.axis_index("x"), 1) == 1
    yl = lax.axis_index("yl")
    co = lax.axis_index("co")
    half = pre_own.shape[0]
    w = w_out[pl.ds(pl.multiple_of((co * 2 + yl) * half, half), half), :]
    unspread = dot(w, dl[...], NN)
    high = unspread.astype(BF16)
    rest = unspread - high.astype(F32)
    middle = rest.astype(BF16)
    terms[:half, :] = high
    terms[half : 2 * half, :] = middle
    terms[2 * half :, :] = (rest - middle.astype(F32)).astype(BF16)
    tiles = tiles_of(dl.shape[1])
    reach = dense.shape[1] // TILE
    share = None
    for block in range(3 * len(tiles)):
        spread = None
        for t, at in tiles:
            if 0 <= block - t < reach:
                part = dot(terms[:, at], dense[at, (block - t) * TILE : (block - t + 1) * TILE], NN)
                spread = part if spread is None else spread + part
        back = spread[:half] + (spread[half : 2 * half] + spread[2 * half :])
        stripe, tile = divmod(block, len(tiles))
        at = tiles[tile][1]
        if stripe == 1:
            v, prop_in = pre_own[:, at], own_in[:, at]
        else:
            is_near = odd if stripe == 0 else jnp.logical_not(odd)
            v = jnp.where(is_near, pre_near[:, at], pre_far[:, at])
            prop_in = jnp.where(is_near, near_in[:, at], far_in[:, at])
        th = jnp.tanh(GELU_A * (v + GELU_B * (v * v * v)))
        slope = 0.5 * (1.0 + th) + (0.5 * v) * (1.0 - th * th) * (
            GELU_A * (1.0 + (3.0 * GELU_B) * (v * v))
        )
        grad = back * slope
        high = grad.astype(BF16)
        low = (grad - high.astype(F32)).astype(BF16)
        part = dot(jnp.concatenate([high, low], axis=0), prop_in, NT)
        share = part if share is None else share + part
    share = share[:half] + share[half:]
    pieces, rows, _ = out.shape
    width = share.shape[1]
    for p in range(pieces):
        out[p, :, :width] = share[p * rows : (p + 1) * rows]
        out[p, :, width:] = share_out[p * rows : (p + 1) * rows]


def sum_kernel(parts, out):
    total = parts[0]
    for p in range(1, parts.shape[0]):
        total = total + parts[p]
    for p in range(out.shape[0]):
        out[p] = total


def collect_kernel(parts, grad_in, grad_out, rows_ref):
    planes = parts.shape[0] // 4
    rows = parts.shape[1]
    width = grad_in.shape[0]
    for p in range(planes):
        for yl in range(2):
            for co in range(2):
                at = ((co * 2 + yl) * planes + p) * rows
                rows_ref[at : at + rows, :] = parts[p * 4 + yl * 2 + co]
    grad_in[...] = rows_ref[:, :width].T
    grad_out[...] = rows_ref[:, width:]


def call(kernel, args, out_shape, mib=16, scratch=()):
    many = isinstance(out_shape, (tuple, list))
    return pl.pallas_call(
        kernel,
        in_specs=[whole()] * len(args),
        out_specs=[whole()] * len(out_shape) if many else whole(),
        out_shape=out_shape,
        scratch_shapes=list(scratch),
        compiler_params=params(mib),
    )(*args)


def halo(value):
    count = lax.axis_size(BLK)
    far = [(i, (i + 1 if i % 2 else i - 1) % count) for i in range(count)]
    far = lax.ppermute(value, BLK, far)
    near = lax.ppermute(value, BLK, [(i, i ^ 1) for i in range(count)])
    return near, far


def start_part(own, piece, dense, near):
    shape = (own.shape[1], own.shape[0])
    return call(functools.partial(start_kernel, near), (own, piece, dense), sds(shape, F32))


def flipped(value, axis):
    shift = {"co": 1, "yl": 2}[axis]
    return lax.ppermute(value, FEAT, [(i, i ^ shift) for i in range(4)])


def on_device(
    features, block_values, block_rows, block_cols, block_count, labels, weight_in, weight_out
):
    devices = lax.axis_size(BLK)
    depth, stripe = features.shape
    node_scale = 1.0 / math.sqrt(devices * stripe)
    hid = weight_in.shape[1]
    classes = weight_out.shape[1]
    mine = labels.shape[0]

    near, far = halo(features)
    dense = assemble(block_values, block_rows, block_cols, block_count, stripe)
    first, plain = call(
        prop_in_kernel,
        (far, start_part(features, near, dense, True), labels.reshape(1, mine), dense),
        (sds((depth + TAG, stripe), BF16), sds((depth, stripe), BF16)),
    )
    near, far = halo(plain)
    third = flipped(first, "yl")
    second = flipped(first, "co")
    fourth = flipped(third, "co")
    both = call(stack_kernel, (near, far), sds((2 * depth, stripe), BF16))
    both_third = flipped(both, "yl")
    both_second = flipped(both, "co")
    both_fourth = flipped(both_third, "co")

    pre = sds((hid // 4, stripe), F32)
    hidden = pltpu.VMEM((hid, stripe), BF16)
    whole_pre = pltpu.VMEM((hid, stripe), F32)
    whole_in = sds((4 * depth, stripe), BF16)
    acc, pre_own, prop_in, label_rows = call(
        own_hidden_kernel,
        (first, second, third, fourth, weight_in, dense),
        (sds((stripe, hid), F32), pre, whole_in, sds((TAG, stripe), F32)),
        scratch=[hidden, whole_pre],
    )
    prop_hid, near_in, far_in, pre_near, pre_far = call(
        prop_hidden_kernel,
        (both, both_second, both_third, both_fourth, weight_in, acc, dense),
        (sds((hid, stripe), BF16), whole_in, whole_in, pre, pre),
        scratch=[hidden, whole_pre, pltpu.VMEM((stripe, hid), F32)],
        mib=24,
    )
    logits, dl, share_out = call(
        functools.partial(logits_kernel, node_scale),
        (prop_hid, weight_out, label_rows),
        (
            sds((classes, mine), F32),
            sds((classes, stripe), BF16),
            sds((hid // 4, classes), F32),
        ),
        scratch=[pltpu.VMEM((classes, stripe), F32)],
    )

    plane = lax.axis_size(PLANE)
    rows = hid // 4 // plane
    width = 4 * depth + classes
    share = call(
        grads_kernel,
        (
            dl,
            dense,
            weight_out,
            pre_own,
            pre_near,
            pre_far,
            prop_in,
            near_in,
            far_in,
            share_out,
        ),
        sds((plane, rows, width), F32),
        scratch=[pltpu.VMEM((3 * hid // 4, stripe), BF16)],
    )
    parts = lax.all_to_all(share, PLANE, 0, 0, tiled=True)
    parts = call(sum_kernel, (parts,), sds((lax.axis_size("z"), rows, width), F32))
    parts = lax.all_to_all(parts, "z", 0, 0, tiled=True)
    parts = call(sum_kernel, (parts,), sds((plane * 4, rows, width), F32))
    parts = lax.all_to_all(parts, PLANE + FEAT, 0, 0, tiled=True)
    grad_in, grad_out = call(
        collect_kernel,
        (parts,),
        (sds((4 * depth, hid), F32), sds((hid, classes), F32)),
        scratch=[pltpu.VMEM((hid, width), F32)],
    )
    return (logits, grad_in, grad_out)


def solution(mesh):
    fine = Mesh(mesh.devices.reshape(2, 16, 4, 2, 2), BLK + FEAT)
    placed = (
        P(FEAT, BLK),
        P(BLK, None, None),
        P(BLK),
        P(BLK),
        P(BLK),
        P(BLK + FEAT),
        P(),
        P(),
    )
    return jax.shard_map(
        on_device,
        mesh=fine,
        in_specs=placed,
        out_specs=(P(None, BLK + FEAT), P(), P()),
        check_vma=False,
    )
```

```python
import functools
import math

import jax
import jax.numpy as jnp
from jax import lax
from jax.experimental import pallas as pl
from jax.experimental.pallas import tpu as pltpu
from jax.sharding import Mesh
from jax.sharding import PartitionSpec as P


BLK = ("yh", "z", "x")
FEAT = ("yl", "co")
PLANE = ("yh", "x")
F32 = jnp.float32
BF16 = jnp.bfloat16
BS = 128
WIDTH = 18 * BS
TILE = 2 * BS
TAG = 8
NT = (((1,), (1,)), ((), ()))
NN = (((1,), (0,)), ((), ()))
TN = (((0,), (0,)), ((), ()))
GELU_A = math.sqrt(2.0 / math.pi)
GELU_B = 0.044715


def dot(a, b, dims):
    return lax.dot_general(a, b, dims, preferred_element_type=F32)


def params(mib):
    return pltpu.CompilerParams(vmem_limit_bytes=mib << 20)


def whole():
    return pl.BlockSpec(memory_space=pltpu.VMEM)


def sds(shape, dtype):
    return jax.ShapeDtypeStruct(shape, dtype)


def assemble_kernel(chunks, rows_ref, cols_ref, count_ref, blocks_hbm, dense_ref, blocks, sems):
    slots = blocks.shape[0]
    each = slots // chunks
    copies = [
        pltpu.make_async_copy(
            blocks_hbm.at[pl.ds(i * each, each)], blocks.at[pl.ds(i * each, each)], sems.at[i]
        )
        for i in range(chunks)
    ]
    for copy in copies:
        copy.start()
    spare = dense_ref.shape[0] - BS
    total_blocks = spare // BS * lax.axis_size(BLK)
    first = (lax.axis_index(BLK) - 1) * (spare // BS)
    count = count_ref[0]
    dense_ref[...] = jnp.zeros_like(dense_ref)
    for i in range(chunks):
        copies[i].wait()

        def place(slot, carry):
            row = rows_ref[slot]
            local = cols_ref[slot] - first
            local = jnp.where(local < 0, local + total_blocks, local)
            local = jnp.where(local >= total_blocks, local - total_blocks, local)
            col = local - row + lax.bitwise_and(row, 1)
            row = jnp.where(slot < count, row * BS, spare)
            row = pl.multiple_of(row, BS)
            col = pl.multiple_of(col * BS, BS)
            dense_ref[pl.ds(row, BS), pl.ds(col, BS)] = blocks[slot]
            return carry

        lax.fori_loop(i * each, (i + 1) * each, place, 0, unroll=True)


def assemble(block_values, rows, cols, count, stripe_rows):
    chunks = 4
    shape = (stripe_rows + BS, WIDTH)
    smem = pl.BlockSpec(memory_space=pltpu.SMEM)
    return pl.pallas_call(
        functools.partial(assemble_kernel, chunks),
        in_specs=[smem, smem, smem, pl.BlockSpec(memory_space=pltpu.HBM)],
        out_specs=whole(),
        out_shape=sds(shape, BF16),
        scratch_shapes=[
            pltpu.VMEM(block_values.shape, BF16),
            pltpu.SemaphoreType.DMA((chunks,)),
        ],
        compiler_params=params(24),
        name="assemble",
    )(in_hbm(rows), in_hbm(cols), count, in_hbm(block_values))


def in_hbm(value):
    return pltpu.with_memory_space_constraint(value, pltpu.HBM)


def tiles_of(stripe):
    return [(t, slice(t * TILE, (t + 1) * TILE)) for t in range(stripe // TILE)]


def on_sides(near, body):
    odd = lax.bitwise_and(lax.axis_index("x"), 1) == 1
    to_left = odd if near else jnp.logical_not(odd)

    @pl.when(to_left)
    def _():
        body(left_product)

    @pl.when(jnp.logical_not(to_left))
    def _():
        body(right_product)


def left_product(dense, piece, t, at):
    return dot(dense[at, : piece.shape[1] - t * TILE], piece[:, t * TILE :], NT)


def right_product(dense, piece, t, at):
    start = 2 * piece.shape[1] - t * TILE
    return dot(dense[at, start:], piece[:, : (t + 1) * TILE], NT)


def own_product(dense, piece, t, at):
    start = piece.shape[1] - t * TILE
    return dot(dense[at, start : start + piece.shape[1]], piece[...], NT)


def start_kernel(near, own, piece, dense, acc):
    def body(product):
        for t, at in tiles_of(own.shape[1]):
            acc[at, :] = own_product(dense, own, t, at) + product(dense, piece, t, at)

    on_sides(near, body)


def prop_in_kernel(far, acc, labels, dense, out, plain):
    channels = far.shape[0]
    tag = jnp.broadcast_to(labels[...].astype(F32), (TAG, labels.shape[1])).astype(BF16)
    for t, at in tiles_of(far.shape[1]):
        out[channels:, at] = tag if t == 0 else jnp.zeros_like(tag)

    def body(product):
        for t, at in tiles_of(far.shape[1]):
            total = acc[at, :] + product(dense, far, t, at)
            value = total.T.astype(BF16)
            out[:channels, at] = value
            plain[:, at] = value

    on_sides(False, body)


def stack_kernel(near, far, both):
    rows = near.shape[0]
    both[:rows, :] = near[...]
    both[rows:, :] = far[...]


def gather(parts, place_part):
    yl = lax.axis_index("yl")
    co = lax.axis_index("co")
    for part, (dy, dc) in zip(parts, ((0, 0), (0, 1), (1, 0), (1, 1))):
        place_part(part, (yl + dy - 2 * yl * dy) * 2 + (co + dc - 2 * co * dc))


def hidden_of(prop_in, w_in, hidden, pre_part, whole_pre):
    yl = lax.axis_index("yl")
    co = lax.axis_index("co")
    pre = dot(w_in[...], prop_in[...], TN)
    inner = GELU_A * (pre + GELU_B * (pre * pre * pre))
    hidden[...] = (pre * (0.5 * (1.0 + jnp.tanh(inner)))).astype(BF16)
    whole_pre[...] = pre
    rows = pre_part.shape[0]
    pre_part[...] = whole_pre[pl.ds(pl.multiple_of((co * 2 + yl) * rows, rows), rows), :]


def own_hidden_kernel(
    first, second, third, fourth, w_in, dense, acc, pre_part, prop_in, labels, hidden, whole_pre
):
    depth = prop_in.shape[0] // 4

    def place_part(part, place):
        prop_in[pl.ds(pl.multiple_of(place * depth, depth), depth), :] = part[:depth, :]
        labels[:, pl.ds(pl.multiple_of(place * TILE, TILE), TILE)] = part[
            depth : depth + TAG, :TILE
        ].astype(F32)

    gather((first, second, third, fourth), place_part)
    hidden_of(prop_in, w_in, hidden, pre_part, whole_pre)
    for t, at in tiles_of(hidden.shape[1]):
        acc[at, :] = own_product(dense, hidden, t, at)


def prop_hidden_kernel(
    first, second, third, fourth, w_in, acc, dense,
    out, near_in, far_in, pre_near, pre_far,
    hidden, whole_pre, total,
):
    depth = near_in.shape[0] // 4

    def place_part(part, place):
        rows = pl.ds(pl.multiple_of(place * depth, depth), depth)
        near_in[rows, :] = part[:depth, :]
        far_in[rows, :] = part[depth:, :]

    gather((first, second, third, fourth), place_part)
    hidden_of(near_in, w_in, hidden, pre_near, whole_pre)

    def add_near(product):
        for t, at in tiles_of(out.shape[1]):
            total[at, :] = acc[at, :] + product(dense, hidden, t, at)

    on_sides(True, add_near)
    hidden_of(far_in, w_in, hidden, pre_far, whole_pre)

    def add_far(product):
        for t, at in tiles_of(out.shape[1]):
            out[:, at] = (total[at, :] + product(dense, hidden, t, at)).T.astype(BF16)

    on_sides(False, add_far)


def logits_kernel(scale, prop_hid, w_out, labels, out, dl, share, scores):
    yl = lax.axis_index("yl")
    co = lax.axis_index("co")
    logit = dot(w_out[...], prop_hid[...], TN)
    scores[...] = logit
    start = pl.multiple_of((yl * 2 + co) * out.shape[1], out.shape[1])
    out[...] = scores[:, pl.ds(start, out.shape[1])]
    shifted = logit - jnp.max(logit, axis=0, keepdims=True)
    exponent = jnp.exp(shifted)
    probability = exponent / jnp.sum(exponent, axis=0, keepdims=True)
    classes = lax.broadcasted_iota(jnp.int32, logit.shape, 0).astype(F32)
    onehot = jnp.where(classes == labels[0:1, :], 1.0, 0.0)
    dlogits = ((probability - onehot) * scale).astype(BF16)
    dl[...] = dlogits
    rows = share.shape[0]
    mine = prop_hid[pl.ds(pl.multiple_of((co * 2 + yl) * rows, rows), rows), :]
    share[...] = dot(mine, dlogits, NT)


def grads_kernel(
    dl, dense, w_out, pre_own, pre_near, pre_far, own_in, near_in, far_in, share_out, out, terms
):
    odd = lax.bitwise_and(lax.axis_index("x"), 1) == 1
    yl = lax.axis_index("yl")
    co = lax.axis_index("co")
    half = pre_own.shape[0]
    w = w_out[pl.ds(pl.multiple_of((co * 2 + yl) * half, half), half), :]
    unspread = dot(w, dl[...], NN)
    high = unspread.astype(BF16)
    rest = unspread - high.astype(F32)
    middle = rest.astype(BF16)
    terms[:half, :] = high
    terms[half : 2 * half, :] = middle
    terms[2 * half :, :] = (rest - middle.astype(F32)).astype(BF16)
    tiles = tiles_of(dl.shape[1])
    reach = dense.shape[1] // TILE
    share = None
    for block in range(3 * len(tiles)):
        spread = None
        for t, at in tiles:
            if 0 <= block - t < reach:
                part = dot(terms[:, at], dense[at, (block - t) * TILE : (block - t + 1) * TILE], NN)
                spread = part if spread is None else spread + part
        back = spread[:half] + (spread[half : 2 * half] + spread[2 * half :])
        stripe, tile = divmod(block, len(tiles))
        at = tiles[tile][1]
        if stripe == 1:
            v, prop_in = pre_own[:, at], own_in[:, at]
        else:
            is_near = odd if stripe == 0 else jnp.logical_not(odd)
            v = jnp.where(is_near, pre_near[:, at], pre_far[:, at])
            prop_in = jnp.where(is_near, near_in[:, at], far_in[:, at])
        th = jnp.tanh(GELU_A * (v + GELU_B * (v * v * v)))
        slope = 0.5 * (1.0 + th) + (0.5 * v) * (1.0 - th * th) * (
            GELU_A * (1.0 + (3.0 * GELU_B) * (v * v))
        )
        grad = back * slope
        high = grad.astype(BF16)
        low = (grad - high.astype(F32)).astype(BF16)
        part = dot(jnp.concatenate([high, low], axis=0), prop_in, NT)
        share = part if share is None else share + part
    share = share[:half] + share[half:]
    pieces, rows, _ = out.shape
    width = share.shape[1]
    for p in range(pieces):
        out[p, :, :width] = share[p * rows : (p + 1) * rows]
        out[p, :, width:] = share_out[p * rows : (p + 1) * rows]


def tail_kernel(
    scale, first, second, third, fourth, w_in, acc, dense, w_out, labels, pre_own, own_in,
    logits, out,
    prop_hid, near_in, far_in, pre_near, pre_far, hidden, whole_pre, total, dl, share, scores, terms,
):
    prop_hidden_kernel(
        first, second, third, fourth, w_in, acc, dense,
        prop_hid, near_in, far_in, pre_near, pre_far, hidden, whole_pre, total,
    )
    logits_kernel(scale, prop_hid, w_out, labels, logits, dl, share, scores)
    grads_kernel(
        dl, dense, w_out, pre_own, pre_near, pre_far, own_in, near_in, far_in, share, out, terms
    )


def sum_kernel(parts, out):
    total = parts[0]
    for p in range(1, parts.shape[0]):
        total = total + parts[p]
    for p in range(out.shape[0]):
        out[p] = total


def collect_kernel(parts, grad_in, grad_out, rows_ref):
    planes = parts.shape[0] // 4
    rows = parts.shape[1]
    width = grad_in.shape[0]
    for p in range(planes):
        for yl in range(2):
            for co in range(2):
                at = ((co * 2 + yl) * planes + p) * rows
                rows_ref[at : at + rows, :] = parts[p * 4 + yl * 2 + co]
    grad_in[...] = rows_ref[:, :width].T
    grad_out[...] = rows_ref[:, width:]


def call(kernel, args, out_shape, mib=16, scratch=()):
    many = isinstance(out_shape, (tuple, list))
    return pl.pallas_call(
        kernel,
        in_specs=[whole()] * len(args),
        out_specs=[whole()] * len(out_shape) if many else whole(),
        out_shape=out_shape,
        scratch_shapes=list(scratch),
        compiler_params=params(mib),
    )(*args)


def halo(value):
    count = lax.axis_size(BLK)
    far = [(i, (i + 1 if i % 2 else i - 1) % count) for i in range(count)]
    far = lax.ppermute(value, BLK, far)
    near = lax.ppermute(value, BLK, [(i, i ^ 1) for i in range(count)])
    return near, far


def start_part(own, piece, dense, near):
    shape = (own.shape[1], own.shape[0])
    return call(functools.partial(start_kernel, near), (own, piece, dense), sds(shape, F32))


def flipped(value, axis):
    shift = {"co": 1, "yl": 2}[axis]
    return lax.ppermute(value, FEAT, [(i, i ^ shift) for i in range(4)])


def on_device(
    features, block_values, block_rows, block_cols, block_count, labels, weight_in, weight_out
):
    devices = lax.axis_size(BLK)
    depth, stripe = features.shape
    node_scale = 1.0 / math.sqrt(devices * stripe)
    hid = weight_in.shape[1]
    classes = weight_out.shape[1]
    mine = labels.shape[0]

    near, far = halo(features)
    dense = assemble(block_values, block_rows, block_cols, block_count, stripe)
    first, plain = call(
        prop_in_kernel,
        (far, start_part(features, near, dense, True), labels.reshape(1, mine), dense),
        (sds((depth + TAG, stripe), BF16), sds((depth, stripe), BF16)),
    )
    near, far = halo(plain)
    third = flipped(first, "yl")
    second = flipped(first, "co")
    fourth = flipped(third, "co")
    both = call(stack_kernel, (near, far), sds((2 * depth, stripe), BF16))
    both_third = flipped(both, "yl")
    both_second = flipped(both, "co")
    both_fourth = flipped(both_third, "co")

    pre = sds((hid // 4, stripe), F32)
    hidden = pltpu.VMEM((hid, stripe), BF16)
    whole_pre = pltpu.VMEM((hid, stripe), F32)
    whole_in = sds((4 * depth, stripe), BF16)
    acc, pre_own, prop_in, label_rows = call(
        own_hidden_kernel,
        (first, second, third, fourth, weight_in, dense),
        (sds((stripe, hid), F32), pre, whole_in, sds((TAG, stripe), F32)),
        scratch=[hidden, whole_pre],
    )
    plane = lax.axis_size(PLANE)
    rows = hid // 4 // plane
    width = 4 * depth + classes
    tail_inputs = (both, both_second, both_third, both_fourth, weight_in, acc, dense)
    logits, share = call(
        functools.partial(tail_kernel, node_scale),
        (*tail_inputs, weight_out, label_rows, pre_own, prop_in),
        (sds((classes, mine), F32), sds((plane, rows, width), F32)),
        mib=32,
        scratch=[
            pltpu.VMEM((hid, stripe), BF16),
            pltpu.VMEM(whole_in.shape, BF16),
            pltpu.VMEM(whole_in.shape, BF16),
            pltpu.VMEM(pre.shape, F32),
            pltpu.VMEM(pre.shape, F32),
            hidden,
            whole_pre,
            pltpu.VMEM((stripe, hid), F32),
            pltpu.VMEM((classes, stripe), BF16),
            pltpu.VMEM((hid // 4, classes), F32),
            pltpu.VMEM((classes, stripe), F32),
            pltpu.VMEM((3 * hid // 4, stripe), BF16),
        ],
    )
    parts = lax.all_to_all(share, PLANE, 0, 0, tiled=True)
    parts = call(sum_kernel, (parts,), sds((lax.axis_size("z"), rows, width), F32))
    parts = lax.all_to_all(parts, "z", 0, 0, tiled=True)
    parts = call(sum_kernel, (parts,), sds((plane * 4, rows, width), F32))
    parts = lax.all_to_all(parts, PLANE + FEAT, 0, 0, tiled=True)
    grad_in, grad_out = call(
        collect_kernel,
        (parts,),
        (sds((4 * depth, hid), F32), sds((hid, classes), F32)),
        scratch=[pltpu.VMEM((hid, width), F32)],
    )
    return (logits, grad_in, grad_out)


def solution(mesh):
    fine = Mesh(mesh.devices.reshape(2, 16, 4, 2, 2), BLK + FEAT)
    placed = (
        P(FEAT, BLK),
        P(BLK, None, None),
        P(BLK),
        P(BLK),
        P(BLK),
        P(BLK + FEAT),
        P(),
        P(),
    )
    return jax.shard_map(
        on_device,
        mesh=fine,
        in_specs=placed,
        out_specs=(P(None, BLK + FEAT), P(), P()),
        check_vma=False,
    )
```

```python
import functools
import math

import jax
import jax.numpy as jnp
from jax import lax
from jax.experimental import pallas as pl
from jax.experimental.pallas import tpu as pltpu
from jax.sharding import Mesh
from jax.sharding import PartitionSpec as P


BLK = ("yh", "zh", "zp", "x")
FEAT = ("yl", "co")
PLANE = ("yh", "zp", "x")
F32 = jnp.float32
BF16 = jnp.bfloat16
BS = 128
WIDTH = 18 * BS
TILE = 2 * BS
TAG = 8
NT = (((1,), (1,)), ((), ()))
NN = (((1,), (0,)), ((), ()))
TN = (((0,), (0,)), ((), ()))
GELU_A = math.sqrt(2.0 / math.pi)
GELU_B = 0.044715


def dot(a, b, dims):
    return lax.dot_general(a, b, dims, preferred_element_type=F32)


def params(mib):
    return pltpu.CompilerParams(vmem_limit_bytes=mib << 20)


def whole():
    return pl.BlockSpec(memory_space=pltpu.VMEM)


def sds(shape, dtype):
    return jax.ShapeDtypeStruct(shape, dtype)


def assemble_kernel(chunks, rows_ref, cols_ref, count_ref, blocks_hbm, dense_ref, blocks, sems):
    slots = blocks.shape[0]
    each = slots // chunks
    copies = [
        pltpu.make_async_copy(
            blocks_hbm.at[pl.ds(i * each, each)], blocks.at[pl.ds(i * each, each)], sems.at[i]
        )
        for i in range(chunks)
    ]
    for copy in copies:
        copy.start()
    spare = dense_ref.shape[0] - BS
    total_blocks = spare // BS * lax.axis_size(BLK)
    first = (lax.axis_index(BLK) - 1) * (spare // BS)
    count = count_ref[0]
    dense_ref[...] = jnp.zeros_like(dense_ref)
    for i in range(chunks):
        copies[i].wait()

        def place(slot, carry):
            row = rows_ref[slot]
            local = cols_ref[slot] - first
            local = jnp.where(local < 0, local + total_blocks, local)
            local = jnp.where(local >= total_blocks, local - total_blocks, local)
            col = local - row + lax.bitwise_and(row, 1)
            row = jnp.where(slot < count, row * BS, spare)
            row = pl.multiple_of(row, BS)
            col = pl.multiple_of(col * BS, BS)
            dense_ref[pl.ds(row, BS), pl.ds(col, BS)] = blocks[slot]
            return carry

        lax.fori_loop(i * each, (i + 1) * each, place, 0, unroll=True)


def assemble(block_values, rows, cols, count, stripe_rows):
    chunks = 4
    shape = (stripe_rows + BS, WIDTH)
    smem = pl.BlockSpec(memory_space=pltpu.SMEM)
    return pl.pallas_call(
        functools.partial(assemble_kernel, chunks),
        in_specs=[smem, smem, smem, pl.BlockSpec(memory_space=pltpu.HBM)],
        out_specs=whole(),
        out_shape=sds(shape, BF16),
        scratch_shapes=[
            pltpu.VMEM(block_values.shape, BF16),
            pltpu.SemaphoreType.DMA((chunks,)),
        ],
        compiler_params=params(24),
        name="assemble",
    )(in_hbm(rows), in_hbm(cols), count, in_hbm(block_values))


def in_hbm(value):
    return pltpu.with_memory_space_constraint(value, pltpu.HBM)


def tiles_of(stripe):
    return [(t, slice(t * TILE, (t + 1) * TILE)) for t in range(stripe // TILE)]


def on_sides(near, body):
    odd = lax.bitwise_and(lax.axis_index("x"), 1) == 1
    to_left = odd if near else jnp.logical_not(odd)

    @pl.when(to_left)
    def _():
        body(left_product)

    @pl.when(jnp.logical_not(to_left))
    def _():
        body(right_product)


def left_product(dense, piece, t, at):
    return dot(dense[at, : piece.shape[1] - t * TILE], piece[:, t * TILE :], NT)


def right_product(dense, piece, t, at):
    start = 2 * piece.shape[1] - t * TILE
    return dot(dense[at, start:], piece[:, : (t + 1) * TILE], NT)


def own_product(dense, piece, t, at):
    start = piece.shape[1] - t * TILE
    return dot(dense[at, start : start + piece.shape[1]], piece[...], NT)


def start_kernel(near, own, piece, dense, acc):
    def body(product):
        for t, at in tiles_of(own.shape[1]):
            acc[at, :] = own_product(dense, own, t, at) + product(dense, piece, t, at)

    on_sides(near, body)


def prop_in_kernel(far, acc, labels, dense, out, plain):
    channels = far.shape[0]
    tag = jnp.broadcast_to(labels[...].astype(F32), (TAG, labels.shape[1])).astype(BF16)
    for t, at in tiles_of(far.shape[1]):
        out[channels:, at] = tag if t == 0 else jnp.zeros_like(tag)

    def body(product):
        for t, at in tiles_of(far.shape[1]):
            total = acc[at, :] + product(dense, far, t, at)
            value = total.T.astype(BF16)
            out[:channels, at] = value
            plain[:, at] = value

    on_sides(False, body)


def stack_kernel(near, far, both):
    rows = near.shape[0]
    both[:rows, :] = near[...]
    both[rows:, :] = far[...]


def gather(parts, place_part):
    yl = lax.axis_index("yl")
    co = lax.axis_index("co")
    for part, (dy, dc) in zip(parts, ((0, 0), (0, 1), (1, 0), (1, 1))):
        place_part(part, (yl + dy - 2 * yl * dy) * 2 + (co + dc - 2 * co * dc))


def hidden_of(prop_in, w_in, hidden, pre_part, whole_pre):
    yl = lax.axis_index("yl")
    co = lax.axis_index("co")
    pre = dot(w_in[...], prop_in[...], TN)
    inner = GELU_A * (pre + GELU_B * (pre * pre * pre))
    hidden[...] = (pre * (0.5 * (1.0 + jnp.tanh(inner)))).astype(BF16)
    whole_pre[...] = pre
    rows = pre_part.shape[0]
    pre_part[...] = whole_pre[pl.ds(pl.multiple_of((co * 2 + yl) * rows, rows), rows), :]


def own_hidden_kernel(
    first, second, third, fourth, w_in, dense, acc, pre_part, prop_in, labels, hidden, whole_pre
):
    depth = prop_in.shape[0] // 4

    def place_part(part, place):
        prop_in[pl.ds(pl.multiple_of(place * depth, depth), depth), :] = part[:depth, :]
        labels[:, pl.ds(pl.multiple_of(place * TILE, TILE), TILE)] = part[
            depth : depth + TAG, :TILE
        ].astype(F32)

    gather((first, second, third, fourth), place_part)
    hidden_of(prop_in, w_in, hidden, pre_part, whole_pre)
    for t, at in tiles_of(hidden.shape[1]):
        acc[at, :] = own_product(dense, hidden, t, at)


def prop_hidden_kernel(
    first, second, third, fourth, w_in, acc, dense,
    out, near_in, far_in, pre_near, pre_far,
    hidden, whole_pre, total,
):
    depth = near_in.shape[0] // 4

    def place_part(part, place):
        rows = pl.ds(pl.multiple_of(place * depth, depth), depth)
        near_in[rows, :] = part[:depth, :]
        far_in[rows, :] = part[depth:, :]

    gather((first, second, third, fourth), place_part)
    hidden_of(near_in, w_in, hidden, pre_near, whole_pre)

    def add_near(product):
        for t, at in tiles_of(out.shape[1]):
            total[at, :] = acc[at, :] + product(dense, hidden, t, at)

    on_sides(True, add_near)
    hidden_of(far_in, w_in, hidden, pre_far, whole_pre)

    def add_far(product):
        for t, at in tiles_of(out.shape[1]):
            out[:, at] = (total[at, :] + product(dense, hidden, t, at)).T.astype(BF16)

    on_sides(False, add_far)


def logits_kernel(scale, prop_hid, w_out, labels, out, dl, share, scores):
    yl = lax.axis_index("yl")
    co = lax.axis_index("co")
    logit = dot(w_out[...], prop_hid[...], TN)
    scores[...] = logit
    start = pl.multiple_of((yl * 2 + co) * out.shape[1], out.shape[1])
    out[...] = scores[:, pl.ds(start, out.shape[1])]
    shifted = logit - jnp.max(logit, axis=0, keepdims=True)
    exponent = jnp.exp(shifted)
    probability = exponent / jnp.sum(exponent, axis=0, keepdims=True)
    classes = lax.broadcasted_iota(jnp.int32, logit.shape, 0).astype(F32)
    onehot = jnp.where(classes == labels[0:1, :], 1.0, 0.0)
    dlogits = ((probability - onehot) * scale).astype(BF16)
    dl[...] = dlogits
    rows = share.shape[0]
    mine = prop_hid[pl.ds(pl.multiple_of((co * 2 + yl) * rows, rows), rows), :]
    share[...] = dot(mine, dlogits, NT)


def grads_kernel(
    dl, dense, w_out, pre_own, pre_near, pre_far, own_in, near_in, far_in, share_out, out, terms
):
    odd = lax.bitwise_and(lax.axis_index("x"), 1) == 1
    yl = lax.axis_index("yl")
    co = lax.axis_index("co")
    half = pre_own.shape[0]
    w = w_out[pl.ds(pl.multiple_of((co * 2 + yl) * half, half), half), :]
    unspread = dot(w, dl[...], NN)
    high = unspread.astype(BF16)
    rest = unspread - high.astype(F32)
    middle = rest.astype(BF16)
    terms[:half, :] = high
    terms[half : 2 * half, :] = middle
    terms[2 * half :, :] = (rest - middle.astype(F32)).astype(BF16)
    tiles = tiles_of(dl.shape[1])
    reach = dense.shape[1] // TILE
    share = None
    for block in range(3 * len(tiles)):
        spread = None
        for t, at in tiles:
            if 0 <= block - t < reach:
                part = dot(terms[:, at], dense[at, (block - t) * TILE : (block - t + 1) * TILE], NN)
                spread = part if spread is None else spread + part
        back = spread[:half] + (spread[half : 2 * half] + spread[2 * half :])
        stripe, tile = divmod(block, len(tiles))
        at = tiles[tile][1]
        if stripe == 1:
            v, prop_in = pre_own[:, at], own_in[:, at]
        else:
            is_near = odd if stripe == 0 else jnp.logical_not(odd)
            v = jnp.where(is_near, pre_near[:, at], pre_far[:, at])
            prop_in = jnp.where(is_near, near_in[:, at], far_in[:, at])
        th = jnp.tanh(GELU_A * (v + GELU_B * (v * v * v)))
        slope = 0.5 * (1.0 + th) + (0.5 * v) * (1.0 - th * th) * (
            GELU_A * (1.0 + (3.0 * GELU_B) * (v * v))
        )
        grad = back * slope
        high = grad.astype(BF16)
        low = (grad - high.astype(F32)).astype(BF16)
        part = dot(jnp.concatenate([high, low], axis=0), prop_in, NT)
        share = part if share is None else share + part
    share = share[:half] + share[half:]
    pieces, rows, _ = out.shape
    width = share.shape[1]
    for p in range(pieces):
        out[p, :, :width] = share[p * rows : (p + 1) * rows]
        out[p, :, width:] = share_out[p * rows : (p + 1) * rows]


def tail_kernel(
    scale, first, second, third, fourth, w_in, acc, dense, w_out, labels, pre_own, own_in,
    logits, out,
    prop_hid, near_in, far_in, pre_near, pre_far, hidden, whole_pre, total, dl, share, scores, terms,
):
    prop_hidden_kernel(
        first, second, third, fourth, w_in, acc, dense,
        prop_hid, near_in, far_in, pre_near, pre_far, hidden, whole_pre, total,
    )
    logits_kernel(scale, prop_hid, w_out, labels, logits, dl, share, scores)
    grads_kernel(
        dl, dense, w_out, pre_own, pre_near, pre_far, own_in, near_in, far_in, share, out, terms
    )


def sum_kernel(parts, out):
    total = parts[0]
    for p in range(1, parts.shape[0]):
        total = total + parts[p]
    for p in range(out.shape[0]):
        out[p] = total


def collect_kernel(parts, grad_in, grad_out, rows_ref):
    planes = parts.shape[0] // 4
    rows = parts.shape[1]
    width = grad_in.shape[0]
    for p in range(planes):
        for yl in range(2):
            for co in range(2):
                at = ((co * 2 + yl) * planes + p) * rows
                rows_ref[at : at + rows, :] = parts[p * 4 + yl * 2 + co]
    grad_in[...] = rows_ref[:, :width].T
    grad_out[...] = rows_ref[:, width:]


def call(kernel, args, out_shape, mib=16, scratch=()):
    many = isinstance(out_shape, (tuple, list))
    return pl.pallas_call(
        kernel,
        in_specs=[whole()] * len(args),
        out_specs=[whole()] * len(out_shape) if many else whole(),
        out_shape=out_shape,
        scratch_shapes=list(scratch),
        compiler_params=params(mib),
    )(*args)


def halo(value):
    count = lax.axis_size(BLK)
    far = [(i, (i + 1 if i % 2 else i - 1) % count) for i in range(count)]
    far = lax.ppermute(value, BLK, far)
    near = lax.ppermute(value, BLK, [(i, i ^ 1) for i in range(count)])
    return near, far


def start_part(own, piece, dense, near):
    shape = (own.shape[1], own.shape[0])
    return call(functools.partial(start_kernel, near), (own, piece, dense), sds(shape, F32))


def flipped(value, axis):
    shift = {"co": 1, "yl": 2}[axis]
    return lax.ppermute(value, FEAT, [(i, i ^ shift) for i in range(4)])


def on_device(
    features, block_values, block_rows, block_cols, block_count, labels, weight_in, weight_out
):
    devices = lax.axis_size(BLK)
    depth, stripe = features.shape
    node_scale = 1.0 / math.sqrt(devices * stripe)
    hid = weight_in.shape[1]
    classes = weight_out.shape[1]
    mine = labels.shape[0]

    near, far = halo(features)
    dense = assemble(block_values, block_rows, block_cols, block_count, stripe)
    first, plain = call(
        prop_in_kernel,
        (far, start_part(features, near, dense, True), labels.reshape(1, mine), dense),
        (sds((depth + TAG, stripe), BF16), sds((depth, stripe), BF16)),
    )
    near, far = halo(plain)
    third = flipped(first, "yl")
    second = flipped(first, "co")
    fourth = flipped(third, "co")
    both = call(stack_kernel, (near, far), sds((2 * depth, stripe), BF16))
    both_third = flipped(both, "yl")
    both_second = flipped(both, "co")
    both_fourth = flipped(both_third, "co")

    pre = sds((hid // 4, stripe), F32)
    hidden = pltpu.VMEM((hid, stripe), BF16)
    whole_pre = pltpu.VMEM((hid, stripe), F32)
    whole_in = sds((4 * depth, stripe), BF16)
    acc, pre_own, prop_in, label_rows = call(
        own_hidden_kernel,
        (first, second, third, fourth, weight_in, dense),
        (sds((stripe, hid), F32), pre, whole_in, sds((TAG, stripe), F32)),
        scratch=[hidden, whole_pre],
    )
    plane = lax.axis_size(PLANE)
    rows = hid // 4 // plane
    width = 4 * depth + classes
    tail_inputs = (both, both_second, both_third, both_fourth, weight_in, acc, dense)
    logits, share = call(
        functools.partial(tail_kernel, node_scale),
        (*tail_inputs, weight_out, label_rows, pre_own, prop_in),
        (sds((classes, mine), F32), sds((plane, rows, width), F32)),
        mib=32,
        scratch=[
            pltpu.VMEM((hid, stripe), BF16),
            pltpu.VMEM(whole_in.shape, BF16),
            pltpu.VMEM(whole_in.shape, BF16),
            pltpu.VMEM(pre.shape, F32),
            pltpu.VMEM(pre.shape, F32),
            hidden,
            whole_pre,
            pltpu.VMEM((stripe, hid), F32),
            pltpu.VMEM((classes, stripe), BF16),
            pltpu.VMEM((hid // 4, classes), F32),
            pltpu.VMEM((classes, stripe), F32),
            pltpu.VMEM((3 * hid // 4, stripe), BF16),
        ],
    )
    parts = lax.all_to_all(share, PLANE, 0, 0, tiled=True)
    parts = call(sum_kernel, (parts,), sds((lax.axis_size("zh"), rows, width), F32))
    parts = lax.all_to_all(parts, "zh", 0, 0, tiled=True)
    parts = call(sum_kernel, (parts,), sds((plane * 4, rows, width), F32))
    parts = lax.all_to_all(parts, PLANE + FEAT, 0, 0, tiled=True)
    grad_in, grad_out = call(
        collect_kernel,
        (parts,),
        (sds((4 * depth, hid), F32), sds((hid, classes), F32)),
        scratch=[pltpu.VMEM((hid, width), F32)],
    )
    return (logits, grad_in, grad_out)


def solution(mesh):
    fine = Mesh(mesh.devices.reshape(2, 8, 2, 4, 2, 2), BLK + FEAT)
    placed = (
        P(FEAT, BLK),
        P(BLK, None, None),
        P(BLK),
        P(BLK),
        P(BLK),
        P(BLK + FEAT),
        P(),
        P(),
    )
    return jax.shard_map(
        on_device,
        mesh=fine,
        in_specs=placed,
        out_specs=(P(None, BLK + FEAT), P(), P()),
        check_vma=False,
    )
```
